32 devices in a mesh: groups: 2 (over y), gy: 4 (over z), gz: 4 (over x, core).
Axes of the slice: x: 2, y: 2, z: 4, core: 2. Of those that a mesh axis runs over, the one named last changes fastest.
Arguments:
- indirect: float32 [4, 512, 32, 512], P('groups', 'gy', 'gz'), parts along dimension 0, may hold values from -6 to 6
- past_indirect: float32 [8, 2, 512, 32, 512], P('groups', None, 'gy', 'gz'), parts along dimension 0, may hold values from -6 to 6
- past_residual: float32 [8, 2, 512, 32, 512], P('groups', None, 'gy', 'gz'), parts along dimension 0, may hold values from -40 to 40
- atom_table: float32 [10, 4, 4, 128], P('groups', 'gy', 'gz'), parts along dimension 0, may hold values from -4 to 512, as said below
- atom_counts: int32 [8, 4], P(('groups', 'gy'), 'gz'), parts along dimension 0, may hold values from 1 to 128, as said below
- chi_amps: float32 [3, 4], replicated, may hold values from -3 to 3
- chi_widths: float32 [4], replicated, may hold values from 0.5 to 4
Outputs:
- new_indirect: float32 [4, 512, 32, 512], P('groups', 'gy', 'gz'), parts along dimension 0
- residual: float32 [4, 512, 32, 512], P('groups', 'gy', 'gz'), parts along dimension 0
The draws below stay inside these ranges and needn't reach their ends.
There are 2 independent parts, one for each index of `groups`. The reference program is written for one: setup_inputs(seed, part) draws one part's arguments, and reference() takes and returns one part's arrays. A program takes and returns all parts, laid end to end along the dimension named above; an argument that names none is the same for every part. Nothing has to cross between parts.
Inputs may be any that keep to these rules, and one draw needn't show every extreme that they name: `atom_counts`: some pencil has exactly 128 live rows in every draw. `atom_table`: each row of pencil (p, q) has its y position in [p * 128, (p + 1) * 128) and its z position in [q * 8, (q + 1) * 8); x positions lie in [0, 512).
All inputs are finite; a program needn't handle non-finite values.
Results may differ from the reference program's by a relative error of at most 0.0003.
Values sent between devices are 32-bit elements; how exact they have to be, the bound alone decides.
A program may use at most 192 MiB of HBM per device.

```python
import math
import jax
import jax.numpy as jnp
from jax import lax

NX = 512
NY = 512
NZ = 32
HIST = 4
ROWS = 128
TERMS = 4
SIGX = 8
PY = 4
PZ = 4
CY = 128
CZ = 8


def draw_atom_table(key, part):
    cells_y = NY // PY
    cells_z = NZ // PZ
    place_x = jax.random.uniform(jax.random.fold_in(key, 11), (PY, PZ, ROWS), jnp.float32, 0.0, NX * 1.0)
    start_y = (jnp.arange(PY) * cells_y).astype(jnp.float32)[:, None, None]
    start_z = (jnp.arange(PZ) * cells_z).astype(jnp.float32)[None, :, None]
    place_y = start_y + jax.random.uniform(jax.random.fold_in(key, 12), (PY, PZ, ROWS), jnp.float32, 0.0, cells_y * 1.0)
    place_z = start_z + jax.random.uniform(jax.random.fold_in(key, 13), (PY, PZ, ROWS), jnp.float32, 0.0, cells_z * 1.0)
    strength = 0.6 * jnp.clip(jax.random.normal(jax.random.fold_in(key, 14), (2, PY, PZ, ROWS), jnp.float32), -6.0, 6.0)
    return jnp.concatenate([place_x[None], place_y[None], place_z[None], strength], 0).astype(jnp.float32)


def draw_atom_counts(key, part):
    base = jax.random.randint(jax.random.fold_in(key, 21), (PY * PZ,), 1, ROWS + 1)
    chosen = jax.random.randint(jax.random.fold_in(key, 22), (), 0, PY * PZ)
    filled = jnp.where(jnp.arange(PY * PZ) == chosen, ROWS, base)
    return filled.reshape(PY, PZ).astype(jnp.int32)


def draw_past_residual(key, part):
    noise = jnp.clip(jax.random.normal(jax.random.fold_in(key, 31), (HIST, 2, NY, NZ, NX), jnp.float32), -6.0, 6.0)
    row_scale = jnp.exp(jax.random.uniform(jax.random.fold_in(key, 32), (HIST, 2, NY, 1, 1), jnp.float32, 0.0, math.log(10.0)))
    ramp = (1.0 + 2.0 * jnp.arange(NY).astype(jnp.float32) / (NY - 1))[None, None, :, None, None]
    return (0.15 * noise * row_scale * ramp).astype(jnp.float32)


def block_levels(key, dims, pieces, least, high):
    def one(dim, parts):
        steps = jax.random.uniform(jax.random.fold_in(jax.random.fold_in(key, 6), dim), (parts,), jnp.float32, least / len(pieces), high / len(pieces))
        return jnp.repeat(jnp.exp(steps), dims[dim] // parts).reshape((-1,) + (1,) * (len(dims) - dim - 1))

    gain = one(*pieces[0])
    for cut in pieces[1:]:
        gain = gain * one(*cut)
    return gain


def scatter_about(rng, extent, scale, most, split=(), dtype=jnp.bfloat16):
    values = jax.random.normal(rng, extent, jnp.float32) * scale
    if len(split) > 0:
        values = block_levels(rng, extent, split, -0.22, 0.18) * values
    return jnp.clip(values, min=-most, max=most).astype(dtype)


def setup_inputs(seed: int = 0, part: int = 0) -> dict:
    keys = jax.random.split(jax.random.key(seed), 8)
    part_splits = jax.random.split(jax.random.fold_in(keys[7], part), 8)
    return {
        "indirect": scatter_about(part_splits[0], (2, NY, NZ, NX), 1.0, 6.0, ((1, 4), (2, 4)), jnp.float32),
        "past_indirect": scatter_about(part_splits[1], (HIST, 2, NY, NZ, NX), 1.0, 6.0, ((2, 4), (3, 4)), jnp.float32),
        "past_residual": draw_past_residual(jax.random.fold_in(jax.random.fold_in(keys[7], part), 71), part),
        "atom_table": draw_atom_table(jax.random.fold_in(jax.random.fold_in(keys[7], part), 71), part),
        "atom_counts": draw_atom_counts(jax.random.fold_in(jax.random.fold_in(keys[7], part), 71), part),
        "chi_amps": scatter_about(keys[5], (3, TERMS), 0.5, 3.0, (), jnp.float32),
        "chi_widths": jnp.clip(jnp.exp(jax.random.uniform(keys[6], (TERMS,), jnp.float32, math.log(0.5), math.log(4.0))), 0.5, 4.0),
    }


PRECISE = lax.Precision.HIGHEST
MIX_STEP = 0.3
BOND_OH = 1.9
BOND_HH = 3.1

def hartley(length):
    position = lax.iota(jnp.int32, length)
    product = position[:, None] * position[None, :] % length
    angle = product.astype(jnp.float32) * (2.0 * math.pi / length)
    return (jnp.cos(angle) + jnp.sin(angle)) / math.sqrt(length)

def wave_squared(position, length):
    folded = jnp.where(2 * position > length, position - length, position)
    scaled = folded.astype(jnp.float32) * (2.0 * math.pi / length)
    return scaled * scaled

def response(wave_square, chi_amps, chi_widths):
    wavenumber = jnp.sqrt(wave_square)
    summed = [jnp.zeros_like(wave_square) for channel in range(3)]
    for which_term in range(chi_widths.shape[0]):
        gaussian_term = jnp.exp(-wave_square * (chi_widths[which_term] * chi_widths[which_term]))
        summed = [summed[channel] + chi_amps[channel, which_term] * gaussian_term for channel in range(3)]
    oxygen = 1.0 + summed[0]
    mixed_site = 2.0 * jnp.sinc(wavenumber * (BOND_OH / math.pi)) + summed[1]
    hydrogen = 2.0 + 2.0 * jnp.sinc(wavenumber * (BOND_HH / math.pi)) + summed[2]
    return (oxygen, mixed_site, hydrogen)

def couple(spectrum, wave_square, chi_amps, chi_widths):
    oxygen, mixed_site, hydrogen = response(wave_square, chi_amps, chi_widths)
    return jnp.stack([oxygen * spectrum[0] + mixed_site * spectrum[1], mixed_site * spectrum[0] + hydrogen * spectrum[1]])

def gaussian(offset, length, spread):
    offset = offset - length * jnp.floor(offset / length + 0.5)
    return jnp.exp(-0.5 * offset * offset / (spread * spread))

def pencil_field(atom_rows, pencil_y, pencil_z, cells_y, cells_z, total_x, total_y, total_z, spread_x):
    cell_y = (pencil_y * cells_y + lax.iota(jnp.int32, cells_y)).astype(jnp.float32)
    cell_z = (pencil_z * cells_z + lax.iota(jnp.int32, cells_z)).astype(jnp.float32)
    cell_x = lax.iota(jnp.int32, total_x).astype(jnp.float32)
    along_y = gaussian(cell_y[:, None] - atom_rows[1][None, :], total_y, 0.5 * cells_y)
    along_z = gaussian(cell_z[:, None] - atom_rows[2][None, :], total_z, 0.5 * cells_z)
    along_x = gaussian(cell_x[:, None] - atom_rows[0][None, :], total_x, spread_x)
    left = atom_rows[3:5][:, None, None, :] * along_y[None, :, None, :] * along_z[None, None, :, :]
    left = left.reshape(2, cells_y * cells_z, atom_rows.shape[1])
    return jnp.einsum('sra,xa->srx', left, along_x, precision=PRECISE)

def potential(atom_table, atom_counts):
    present = (lax.iota(jnp.int32, ROWS)[None, None, :] < atom_counts[:, :, None]).astype(jnp.float32)
    bucket = jnp.concatenate([atom_table[0:3], atom_table[3:5] * present[None]], 0)
    nearby = []
    for shift_y in (-1, 0, 1):
        for shift_z in (-1, 0, 1):
            nearby.append(jnp.roll(bucket, (-shift_y, -shift_z), (1, 2)))
    nearby = jnp.concatenate(nearby, 3)
    flattened = jnp.transpose(nearby.reshape(5, PY * PZ, 9 * ROWS), (1, 0, 2))

    def per_pencil(inputs):
        atom_rows, pencil = inputs
        return pencil_field(atom_rows, pencil // PZ, pencil % PZ, CY, CZ, NX, NY, NZ, float(SIGX))
    fields = lax.map(per_pencil, (flattened, lax.iota(jnp.int32, PY * PZ)))
    fields = fields.reshape(PY, PZ, 2, CY, CZ, NX)
    return jnp.transpose(fields, (2, 0, 3, 1, 4, 5)).reshape(2, NY, NZ, NX)

def transform(field, table_x, table_y, table_z):
    result = jnp.einsum('syzx,xk->syzk', field, table_x, precision=PRECISE)
    result = jnp.einsum('syzx,yk->skzx', result, table_y, precision=PRECISE)
    return jnp.einsum('syzx,zk->sykx', result, table_z, precision=PRECISE)

def reference(indirect, past_indirect, past_residual, atom_table, atom_counts, chi_amps, chi_widths):
    potential_field = potential(atom_table, atom_counts)
    argument = indirect - potential_field
    closed = jnp.where(argument > 0, argument, jnp.expm1(jnp.minimum(argument, 0.0)))
    direct = closed - indirect
    table_x = hartley(NX)
    table_y = hartley(NY)
    table_z = hartley(NZ)
    spectrum = transform(direct, table_x, table_y, table_z)
    wave_square = wave_squared(lax.iota(jnp.int32, NY), NY)[:, None, None] + wave_squared(lax.iota(jnp.int32, NZ), NZ)[None, :, None] + wave_squared(lax.iota(jnp.int32, NX), NX)[None, None, :]
    coupled = couple(spectrum, wave_square, chi_amps, chi_widths)
    summed_field = transform(coupled, table_x, table_y, table_z)
    residual = summed_field - direct - indirect
    fields = [residual] + [past_residual[member] for member in range(HIST)]
    gram_matrix = jnp.stack([jnp.stack([jnp.sum(first_field * other) for other in fields]) for first_field in fields])
    factor = jnp.linalg.cholesky(gram_matrix)
    weights = jax.scipy.linalg.cho_solve((factor, True), jnp.ones((HIST + 1,), jnp.float32))
    mixing = weights / jnp.sum(weights)
    iterates = [indirect] + [past_indirect[member] for member in range(HIST)]
    new_indirect = jnp.zeros_like(indirect)
    for member in range(HIST + 1):
        new_indirect = new_indirect + mixing[member] * (iterates[member] + MIX_STEP * fields[member])
    return (new_indirect, residual)
```

```python
import functools
import math

import jax
import jax.numpy as jnp
import ml_dtypes
import numpy as np
from jax import lax
from jax.experimental import pallas as pl
from jax.experimental.pallas import tpu as pltpu
from jax.sharding import PartitionSpec as P

SIGX = 8


PRECISE = lax.Precision.HIGH
MIX_STEP = 0.3
BOND_OH = 1.9
BOND_HH = 3.1


def with_halo(cells, sides, width):
    for axis, dim in sides:
        count = lax.axis_size(axis)
        head = lax.slice_in_dim(cells, 0, width, axis=dim)
        tail = lax.slice_in_dim(cells, cells.shape[dim] - width, cells.shape[dim], axis=dim)
        cells = jnp.concatenate(
            [
                lax.ppermute(tail, axis, [(i, (i + 1) % count) for i in range(count)]),
                cells,
                lax.ppermute(head, axis, [((i + 1) % count, i) for i in range(count)]),
            ],
            axis=dim,
        )
    return cells


def hartley(length):
    position = lax.iota(jnp.int32, length)
    product = position[:, None] * position[None, :] % length
    angle = product.astype(jnp.float32) * (2.0 * math.pi / length)
    return (jnp.cos(angle) + jnp.sin(angle)) / math.sqrt(length)


def wave_squared(position, length):
    folded = jnp.where(2 * position > length, position - length, position)
    scaled = folded.astype(jnp.float32) * (2.0 * math.pi / length)
    return scaled * scaled


def response(wave_square, chi_amps, chi_widths):
    wavenumber = jnp.sqrt(wave_square)
    summed = [jnp.zeros_like(wave_square) for channel in range(3)]
    for which_term in range(chi_widths.shape[0]):
        gaussian_term = jnp.exp(-wave_square * (chi_widths[which_term] * chi_widths[which_term]))
        summed = [
            summed[channel] + chi_amps[channel, which_term] * gaussian_term for channel in range(3)
        ]
    oxygen = 1.0 + summed[0]
    mixed_site = 2.0 * jnp.sinc(wavenumber * (BOND_OH / math.pi)) + summed[1]
    hydrogen = 2.0 + 2.0 * jnp.sinc(wavenumber * (BOND_HH / math.pi)) + summed[2]
    return (oxygen, mixed_site, hydrogen)


def gaussian(offset, length, spread):
    offset = offset - length * jnp.floor(offset / length + 0.5)
    return jnp.exp(-0.5 * offset * offset / (spread * spread))


def pencil_field(
    atom_rows, pencil_y, pencil_z, cells_y, cells_z, total_x, total_y, total_z, spread_x
):
    cell_y = (pencil_y * cells_y + lax.iota(jnp.int32, cells_y)).astype(jnp.float32)
    cell_z = (pencil_z * cells_z + lax.iota(jnp.int32, cells_z)).astype(jnp.float32)
    cell_x = lax.iota(jnp.int32, total_x).astype(jnp.float32)
    along_y = gaussian(cell_y[:, None] - atom_rows[1][None, :], total_y, 0.5 * cells_y)
    along_z = gaussian(cell_z[:, None] - atom_rows[2][None, :], total_z, 0.5 * cells_z)
    along_x = gaussian(cell_x[:, None] - atom_rows[0][None, :], total_x, spread_x)
    left = atom_rows[3:5][:, None, None, :] * along_y[None, :, None, :] * along_z[None, None, :, :]
    left = left.reshape(2, cells_y * cells_z, atom_rows.shape[1])
    return jnp.einsum("sra,xa->srx", left, along_x, precision=PRECISE)


def pairs(count):
    return [(i, j) for i in range(count) for j in range(i, count)]


def everywhere(value, axes):
    for axis in axes:
        size = lax.axis_size(axis)
        if size & (size - 1):
            value = lax.psum(value, axis)
            continue
        step = 1
        while step < size:
            value = value + lax.ppermute(value, axis, [(i, i ^ step) for i in range(size)])
            step *= 2
    return value


def finish_kernel(total, direct, indirect, past, residual, products):
    history, _, rows, _, cells_x = past.shape
    couples = pairs(history + 1)

    @pl.when((pl.program_id(0) == 0) & (pl.program_id(1) == 0))
    def _():
        products[...] = jnp.zeros_like(products)

    lanes = products.shape[2]
    sums = tuple(products[n] for n in range(len(couples)))
    for lane in range(0, cells_x, lanes):
        columns = pl.ds(lane, lanes)

        def step(group, sums):
            first = pl.multiple_of(group * 8, 8)
            turned = jnp.swapaxes(total[0, :, pl.ds(first, 8), columns], 0, 1)
            for offset in range(8):
                row = first + offset
                now = turned[offset] - direct[0, row, :, columns] - indirect[0, row, :, columns]
                residual[0, row, :, columns] = now
                values = [now] + [past[h, 0, row, :, columns] for h in range(history)]
                sums = tuple(
                    sums[n] + values[i] * values[j] for n, (i, j) in enumerate(couples)
                )
            return sums

        sums = lax.fori_loop(0, rows // 8, step, sums)
    for n in range(len(couples)):
        products[n] = sums[n]


def block_rows(cells_y):
    return math.gcd(cells_y, 32)


def finish(total, direct, indirect, past_residual):
    history, sites, cells_y, cells_z, cells_x = past_residual.shape
    rows = block_rows(cells_y)
    field = pl.BlockSpec((1, rows, cells_z, cells_x), lambda s, c: (s, c, 0, 0))
    earlier = pl.BlockSpec((history, 1, rows, cells_z, cells_x), lambda s, c: (0, s, c, 0, 0))
    count = len(pairs(history + 1))
    lanes = min(cells_x, 128)
    return pl.pallas_call(
        finish_kernel,
        grid=(sites, cells_y // rows),
        in_specs=[
            pl.BlockSpec((1, cells_z, rows, cells_x), lambda s, c: (s, 0, c, 0)),
            field,
            field,
            earlier,
        ],
        out_specs=[field, pl.BlockSpec((count, cells_z, lanes), lambda s, c: (0, 0, 0))],
        out_shape=[
            jax.ShapeDtypeStruct(indirect.shape, jnp.float32),
            jax.ShapeDtypeStruct((count, cells_z, lanes), jnp.float32),
        ],
        name="finish",
    )(total, direct, indirect, past_residual)


def mix_kernel(mixing, indirect, residual, earlier, out):
    history = earlier.shape[0]
    rows = indirect.shape[1]
    scale = [mixing[h] for h in range(history + 1)]

    def step(row, carry):
        mixed = scale[0] * (indirect[0, row] + MIX_STEP * residual[0, row])
        for h in range(history):
            mixed = mixed + scale[h + 1] * earlier[h, 0, row]
        out[0, row] = mixed
        return carry

    lax.fori_loop(0, rows, step, 0, unroll=2)


def mix(mixing, indirect, residual, earlier):
    history, sites, cells_y, cells_z, cells_x = earlier.shape
    rows = block_rows(cells_y)
    field = pl.BlockSpec((1, rows, cells_z, cells_x), lambda s, c: (s, c, 0, 0))
    stack = pl.BlockSpec((history, 1, rows, cells_z, cells_x), lambda s, c: (0, s, c, 0, 0))
    return pl.pallas_call(
        mix_kernel,
        grid=(sites, cells_y // rows),
        in_specs=[pl.BlockSpec(memory_space=pltpu.SMEM), field, field, stack],
        out_specs=field,
        out_shape=jax.ShapeDtypeStruct(indirect.shape, jnp.float32),
        name="mix",
    )(mixing, indirect, residual, earlier)


def folded_angle(position, length):
    folded = jnp.where(2 * position > length, position - length, position)
    return folded.astype(jnp.float32) * (2.0 * math.pi / length)


def halves(value):
    high = value.astype(jnp.bfloat16)
    return high, (value - high.astype(jnp.float32)).astype(jnp.bfloat16)


def table_halves(table):
    high = table.astype(ml_dtypes.bfloat16)
    return high, (table - high.astype(np.float32)).astype(ml_dtypes.bfloat16)


def product(left, right, dims=(1, 0)):
    numbers = (((dims[0],), (dims[1],)), ((), ()))

    def dot(a, b):
        return lax.dot_general(a, b, numbers, preferred_element_type=jnp.float32)

    return dot(left[0], right[0]) + (dot(left[0], right[1]) + dot(left[1], right[0]))


def host_hartley(length):
    position = np.arange(length)
    angle = (position[:, None] * position[None, :] % length) * (2.0 * math.pi / length)
    return ((np.cos(angle) + np.sin(angle)) / math.sqrt(length)).astype(np.float32)


def sine_over(v):
    turns = jnp.floor(v * (1.0 / math.pi) + 0.5)
    r = (v - turns * 3.140625) - turns * (math.pi - 3.140625)
    odd = turns - 2.0 * jnp.floor(0.5 * turns)
    r2 = r * r
    series = -2.5052108e-08
    for term in (2.7557319e-06, -1.9841270e-04, 8.3333333e-03, -1.6666667e-01):
        series = series * r2 + term
    sine = (r + r * r2 * series) * (1.0 - 2.0 * odd)
    return jnp.where(v == 0.0, 1.0, sine / jnp.where(v == 0.0, 1.0, v))


def solve_ones(gram, count):
    rows = [[gram[min(i, j), max(i, j)] for j in range(count)] for i in range(count)]
    right = [jnp.ones_like(rows[0][0]) for i in range(count)]
    for k in range(count):
        inverse = 1.0 / rows[k][k]
        for i in range(k + 1, count):
            factor = rows[k][i] * inverse
            for j in range(i, count):
                rows[i][j] = rows[i][j] - factor * rows[k][j]
            right[i] = right[i] - factor * right[k]
    weights = [None] * count
    for k in reversed(range(count)):
        value = right[k]
        for j in range(k + 1, count):
            value = value - rows[k][j] * weights[j]
        weights[k] = value / rows[k][k]
    total = weights[0]
    for k in range(1, count):
        total = total + weights[k]
    return [weight / total for weight in weights]


SUB = 8
LANES = 128
AHEAD = 2


def iterate_kernel(
    sizes,
    atoms,
    live,
    amps,
    widths,
    indirect,
    past_indirect,
    past_residual,
    hx_hi,
    hx_lo,
    hb_hi,
    hb_lo,
    hy_hi,
    hy_lo,
    kz_hi,
    kz_lo,
    residual_out,
    earlier_out,
    mixing_out,
    near,
    grid_x,
    grid_y,
    field,
    old,
    outgoing,
    planes,
    returned,
    total,
    spectrum,
    piece,
    sums,
    sums_past,
    near_send,
    near_recv,
    go_send,
    go_recv,
    go_own,
    back_send,
    back_recv,
    back_own,
    sum_send,
    sum_recv,
    past_send,
    past_recv,
    load_sem,
    old_sem,
    in_sem,
    out_sem,
    result_sem,
):
    parts_y, parts_z, sites, cells_y, cells_z, cells_x, history = sizes
    total_y, total_z = parts_y * cells_y, parts_z * cells_z
    blocks = parts_y * parts_z
    width = cells_x // blocks
    chunks = width // SUB
    lines = sites * cells_y
    group = lax.axis_index("groups")
    my_y = lax.axis_index("gy")
    my_z = lax.axis_index("gz")
    me = my_y * parts_z + my_z

    def device(q):
        return (group, q // parts_z, q % parts_z)

    def partner(i):
        return (me + i) % blocks

    def remote(source, target, send, receive, q):
        return pltpu.make_async_remote_copy(
            src_ref=source,
            dst_ref=target,
            send_sem=send,
            recv_sem=receive,
            device_id=device(q),
            device_id_type=pl.DeviceIdType.MESH,
        )

    def each_partner(do):
        def step(i, carry):
            do(partner(i))
            return carry

        lax.fori_loop(1, blocks, step, 0)

    strips = cells_x // LANES
    cells = indirect.shape[0]

    def strip(n):
        return slice(n * LANES, (n + 1) * LANES)

    loads = [
        pltpu.make_async_copy(indirect.at[:, strip(n)], field.at[n], load_sem.at[n])
        for n in range(strips)
    ]
    for load in loads:
        load.start()

    barrier = pltpu.get_barrier_semaphore()
    each_partner(
        lambda q: pl.semaphore_signal(
            barrier, inc=1, device_id=device(q), device_id_type=pl.DeviceIdType.MESH
        )
    )

    rows = atoms.shape[1]
    present = jnp.where(lax.broadcasted_iota(jnp.int32, (2, rows), 1) < live[0, 0], 1.0, 0.0)
    near[4, 0:3, :] = atoms[0:3, :]
    near[4, 3:5, :] = atoms[3:5, :] * present
    near[4, 5:8, :] = jnp.zeros((3, rows), jnp.float32)
    pl.semaphore_wait(barrier, blocks - 1)

    shifts = [(a, b) for a in (-1, 0, 1) for b in (-1, 0, 1)]
    halo = []
    for n, (a, b) in enumerate(shifts):
        if (a, b) != (0, 0):
            q = ((my_y + a + parts_y) % parts_y) * parts_z + (my_z + b + parts_z) % parts_z
            slot = len(shifts) - 1 - n
            halo.append(
                remote(near.at[4], near.at[slot], near_send.at[n], near_recv.at[slot], q)
            )
            halo[-1].start()
    old_load = pltpu.make_async_copy(past_residual, old, old_sem)
    old_load.start()
    for n in range(len(shifts)):
        if n != 4:
            remote(near.at[4], near.at[n], near_send.at[n], near_recv.at[n], me).wait_recv()

    cell_x = lax.broadcasted_iota(jnp.int32, (cells_x, rows), 0).astype(jnp.float32)
    cell_y = (
        my_y * cells_y + lax.broadcasted_iota(jnp.int32, (cells_y, rows), 0)
    ).astype(jnp.float32)

    def near_step(n, carry):
        columns = pl.ds(pl.multiple_of(n * rows, rows), rows)
        along_x = gaussian(cell_x - near[n, 0:1, :], cells_x, float(SIGX))
        high, low = halves(along_x)
        grid_x[0, :, columns] = high
        grid_x[1, :, columns] = low
        grid_y[:, columns] = gaussian(cell_y - near[n, 1:2, :], total_y, 0.5 * cells_y)
        return carry

    lax.fori_loop(0, len(shifts), near_step, 0)
    place_z = jnp.concatenate([near[n, 2:3, :] for n in range(len(shifts))], 1)
    strength = [
        jnp.concatenate([near[n, 3 + s : 4 + s, :] for n in range(len(shifts))], 1)
        for s in range(sites)
    ]
    for load in loads:
        load.wait()

    def go(j, q):
        return remote(
            outgoing.at[j, q], planes.at[j, me], go_send.at[j, q], go_recv.at[j, me], q
        )

    def go_first(d, q):
        return remote(
            outgoing.at[0, q, d], planes.at[0, me, d], go_send.at[0, q], go_recv.at[0, me], q
        )

    def own(j):
        return pltpu.make_async_copy(outgoing.at[j, me], planes.at[j, me], go_own.at[j])

    def slab(d, carry):
        here_z = (my_z * cells_z + d).astype(jnp.float32)
        along_z = gaussian(here_z - place_z, total_z, 0.5 * cells_z)
        left = jnp.concatenate([grid_y[...] * (strength[s] * along_z) for s in range(sites)], 0)
        potential = product(halves(left), (grid_x[0], grid_x[1]), (1, 1))
        now = jnp.concatenate(
            [field[n, pl.ds(d, lines, stride=cells_z), :] for n in range(strips)], 1
        )
        argument = now - potential
        closed = jnp.where(argument > 0, argument, jnp.exp(jnp.minimum(argument, 0.0)) - 1.0)
        total[d] = -closed
        waves = product((hx_hi[...], hx_lo[...]), halves(closed - now), (1, 1))
        for s in range(sites):
            part = waves[:, s * cells_y : (s + 1) * cells_y]
            part = part.reshape(blocks, chunks, SUB, cells_y)
            for j in range(chunks):
                outgoing[j, :, d, s] = part[:, j]
        each_partner(lambda q: go_first(d, q).start())
        return carry

    lax.fori_loop(0, cells_z, slab, 0)
    own(0).start()

    def issue(j):
        own(j).start()
        each_partner(lambda q: go(j, q).start())

    for j in range(1, min(AHEAD, chunks)):
        issue(j)

    old_load.wait()
    couples = pairs(history)
    tall = piece.shape[2]
    pieces = cells // tall

    def piece_in(p):
        return pltpu.make_async_copy(
            past_indirect.at[:, pl.ds(p * tall, tall)], piece.at[p % 3], in_sem.at[p % 3]
        )

    def piece_out(p):
        return pltpu.make_async_copy(
            piece.at[p % 3], earlier_out.at[:, pl.ds(p * tall, tall)], out_sem.at[p % 3]
        )

    def fold(value):
        return jnp.sum(value.reshape(value.shape[0] // SUB, SUB, value.shape[1]), 0)

    def piece_step(p, acc):
        @pl.when(p + 1 < pieces)
        def _():
            @pl.when(p >= 2)
            def _():
                piece_out(p - 2).wait()

            piece_in(p + 1).start()

        piece_in(p).wait()
        slot = p % 3

        def stripe(t, acc):
            place = pl.ds(pl.multiple_of(t * SUB, SUB), SUB)
            from_old = pl.ds(pl.multiple_of(p * tall + t * SUB, SUB), SUB)
            values = [old[h, from_old, :] for h in range(history)]
            for h in range(history):
                piece[slot, h, place, :] = piece[slot, h, place, :] + MIX_STEP * values[h]
            products = []
            for n, (i, j) in enumerate(couples):
                both = values[i] * values[j]
                flat = both[:, 0:LANES]
                for lane in range(LANES, cells_x, LANES):
                    flat = flat + both[:, lane : lane + LANES]
                products.append(acc[n] + flat)
            return tuple(products)

        acc = lax.fori_loop(0, tall // SUB, stripe, acc)
        piece_out(p).start()
        return acc

    piece_in(0).start()
    zero = jnp.zeros((SUB, LANES), jnp.float32)
    acc = lax.fori_loop(0, pieces, piece_step, tuple(zero for _ in couples))
    for p in range(max(0, pieces - 3), pieces):
        piece_out(p).wait()

    def spread(value):
        return jnp.broadcast_to(jnp.sum(value).reshape(1, 1), (1, LANES))

    def put(target, values):
        for n, value in enumerate(values):
            target[me, n : n + 1, :] = spread(value)
        if len(values) < target.shape[1]:
            target[me, len(values) :, :] = jnp.zeros(
                (target.shape[1] - len(values), LANES), jnp.float32
            )

    put(sums_past, acc)

    def share_past(q):
        return remote(sums_past.at[me], sums_past.at[me], past_send.at[q], past_recv.at[me], q)

    each_partner(lambda q: share_past(q).start())

    def couple_step(t, j):
        tall_z = 4 * SUB
        first = pl.multiple_of(t * tall_z, tall_z)
        row = lax.broadcasted_iota(jnp.int32, (tall_z, total_y), 0)
        angle_z = folded_angle((first + row) // SUB, total_z)
        angle_x = folded_angle(me * width + j * SUB + row % SUB, cells_x)
        angle_y = folded_angle(lax.broadcasted_iota(jnp.int32, (tall_z, total_y), 1), total_y)
        square = angle_x * angle_x + angle_z * angle_z + angle_y * angle_y
        number = jnp.sqrt(square)
        oxygen = jnp.ones_like(square)
        mixed = 2.0 * sine_over(number * BOND_OH)
        hydrogen = 2.0 + 2.0 * sine_over(number * BOND_HH)
        for term in range(widths.shape[0]):
            bell = jnp.exp(-square * (widths[term] * widths[term]))
            oxygen = oxygen + amps[0, term] * bell
            mixed = mixed + amps[1, term] * bell
            hydrogen = hydrogen + amps[2, term] * bell
        at = pl.ds(first, tall_z)
        first_site, second_site = spectrum[0, at, :], spectrum[1, at, :]
        spectrum[0, at, :] = oxygen * first_site + mixed * second_site
        spectrum[1, at, :] = mixed * first_site + hydrogen * second_site
        return j

    deep = total_z * SUB

    def middle(j):
        along_y = (hy_hi[...], hy_lo[...])
        along_z = (kz_hi[...], kz_lo[...])
        for s in range(sites):
            plane = jnp.concatenate(
                [
                    planes[j, a * parts_z : (a + 1) * parts_z, :, s].reshape(deep, cells_y)
                    for a in range(parts_y)
                ],
                1,
            )
            plane = product(halves(plane), along_y)
            spectrum[s] = product(along_z, halves(plane))
        lax.fori_loop(0, deep // (4 * SUB), couple_step, j)
        for s in range(sites):
            plane = product(along_z, halves(spectrum[s]))
            plane = product(halves(plane), along_y)
            for a in range(parts_y):
                part = plane[:, a * cells_y : (a + 1) * cells_y]
                planes[j, a * parts_z : (a + 1) * parts_z, :, s] = part.reshape(
                    parts_z, cells_z, SUB, cells_y
                )

    def back(j, q):
        return remote(
            planes.at[j, q], returned.at[j, me], back_send.at[j, q], back_recv.at[j, me], q
        )

    def back_self(j):
        return pltpu.make_async_copy(planes.at[j, me], returned.at[j, me], back_own.at[j])

    def middle_step(j, carry):
        @pl.when(j + AHEAD < chunks)
        def _():
            issue(j + AHEAD)

        own(j).wait()
        each_partner(
            lambda q: remote(
                outgoing.at[j, q], planes.at[j, q], go_send.at[j, q], go_recv.at[j, q], q
            ).wait_recv()
        )
        middle(j)
        back_self(j).start()
        each_partner(lambda q: back(j, q).start())
        return carry

    lax.fori_loop(0, chunks, middle_step, 0)

    def wait_back(j):
        back_self(j).wait()
        each_partner(
            lambda q: remote(
                planes.at[j, q], returned.at[j, q], back_send.at[j, q], back_recv.at[j, q], q
            ).wait_recv()
        )

    def lines_of(j, d):
        waves = jnp.concatenate(
            [returned[j, :, d, s].reshape(blocks * SUB, cells_y) for s in range(sites)], 1
        )
        return product(halves(waves.T), (hb_hi[j], hb_lo[j]))

    def home(j, carry):
        wait_back(j)

        def slab_back(d, carry):
            total[d] = total[d] + lines_of(j, d)
            return carry

        return lax.fori_loop(0, cells_z, slab_back, carry)

    lax.fori_loop(0, chunks - 1, home, 0)
    wait_back(chunks - 1)

    def slab_last(d, carry):
        last = total[d] + lines_of(chunks - 1, d)
        for n in range(strips):
            field[n, pl.ds(d, lines, stride=cells_z), :] = last[:, strip(n)]
        return carry

    lax.fori_loop(0, cells_z, slab_last, 0)
    results = [
        pltpu.make_async_copy(field.at[n], residual_out.at[:, strip(n)], result_sem.at[n])
        for n in range(strips)
    ]
    for result in results:
        result.start()

    def stripe_new(t, acc):
        place = pl.ds(pl.multiple_of(t * SUB, SUB), SUB)
        acc = list(acc)
        for n in range(strips):
            now = field[n, place, :]
            acc[0] = acc[0] + now * now
            for h in range(history):
                acc[h + 1] = acc[h + 1] + now * old[h, place, strip(n)]
        return tuple(acc)

    acc = lax.fori_loop(
        0, cells // SUB, stripe_new, tuple(zero for _ in range(history + 1)), unroll=4
    )
    put(sums, acc)

    def share(q):
        return remote(sums.at[me], sums.at[me], sum_send.at[q], sum_recv.at[me], q)

    each_partner(lambda q: share(q).start())
    each_partner(
        lambda q: remote(
            sums_past.at[me], sums_past.at[q], past_send.at[q], past_recv.at[q], q
        ).wait_recv()
    )
    known = jnp.sum(sums_past[...], 0)
    each_partner(
        lambda q: remote(sums.at[me], sums.at[q], sum_send.at[q], sum_recv.at[q], q).wait_recv()
    )
    fresh = jnp.sum(sums[...], 0)
    gram = {(0, i): fresh[i : i + 1, :] for i in range(history + 1)}
    for n, (i, j) in enumerate(couples):
        gram[i + 1, j + 1] = known[n : n + 1, :]
    for n, value in enumerate(solve_ones(gram, history + 1)):
        mixing_out[n : n + 1, :] = value
    mixing_out[history + 1 :, :] = jnp.zeros(
        (mixing_out.shape[0] - history - 1, LANES), jnp.float32
    )

    for copy in halo:
        copy.wait_send()

    def drain(q):
        share(q).wait_send()
        share_past(q).wait_send()

        def step(j, carry):
            go(j, q).wait_send()
            back(j, q).wait_send()
            return carry

        lax.fori_loop(0, chunks, step, 0)

    each_partner(drain)
    for result in results:
        result.wait()


def fits(sizes, rows):
    parts_y, parts_z, sites, cells_y, cells_z, cells_x, history = sizes
    blocks = parts_y * parts_z
    return (
        min(parts_y, parts_z) >= 3
        and sites == 2
        and cells_y == LANES
        and cells_z % SUB == 0
        and cells_x % LANES == 0
        and cells_x % (blocks * SUB) == 0
        and rows % LANES == 0
        and history + 1 <= SUB
        and history * sites * cells_y * cells_z * cells_x * 4 <= 16 * 2**20
    )


def up(count):
    return -(-count // SUB) * SUB


def iterate(sizes, indirect, past_indirect, past_residual, atom_table, atom_counts, amps, widths):
    parts_y, parts_z, sites, cells_y, cells_z, cells_x, history = sizes
    total_y, total_z = parts_y * cells_y, parts_z * cells_z
    blocks = parts_y * parts_z
    chunks = cells_x // blocks // SUB
    rows = atom_table.shape[3]
    table_x = host_hartley(cells_x)
    table_back = table_x.reshape(blocks, chunks, SUB, cells_x).transpose(1, 0, 2, 3)
    tables = [
        jnp.asarray(half)
        for table in (
            table_x,
            table_back.reshape(chunks, blocks * SUB, cells_x),
            host_hartley(total_y),
            np.kron(host_hartley(total_z), np.eye(SUB, dtype=np.float32)),
        )
        for half in table_halves(table)
    ]
    flat = (sites * cells_y * cells_z, cells_x)
    block = (chunks, blocks, cells_z, sites, SUB, cells_y)
    anywhere = pl.BlockSpec(memory_space=pl.ANY)
    vector = pl.BlockSpec(memory_space=pltpu.VMEM)
    scalar = pl.BlockSpec(memory_space=pltpu.SMEM)
    dma = pltpu.SemaphoreType.DMA
    f32 = jnp.float32
    tall = math.gcd(flat[0], 64)
    residual, earlier, mixing = pl.pallas_call(
        functools.partial(iterate_kernel, sizes),
        in_specs=[vector, scalar, scalar, scalar] + [anywhere] * 3 + [vector] * len(tables),
        out_specs=[anywhere, anywhere, vector],
        out_shape=[
            jax.ShapeDtypeStruct(flat, f32),
            jax.ShapeDtypeStruct((history,) + flat, f32),
            jax.ShapeDtypeStruct((SUB, LANES), f32),
        ],
        scratch_shapes=[
            pltpu.VMEM((9, SUB, rows), f32),
            pltpu.VMEM((2, cells_x, 9 * rows), jnp.bfloat16),
            pltpu.VMEM((cells_y, 9 * rows), f32),
            pltpu.VMEM((cells_x // LANES, flat[0], LANES), f32),
            pltpu.VMEM((history,) + flat, f32),
            pltpu.VMEM(block, f32),
            pltpu.VMEM(block, f32),
            pltpu.VMEM(block, f32),
            pltpu.VMEM((cells_z, sites * cells_y, cells_x), f32),
            pltpu.VMEM((sites, total_z * SUB, total_y), f32),
            pltpu.VMEM((3, history, tall, cells_x), f32),
            pltpu.VMEM((blocks, SUB, LANES), f32),
            pltpu.VMEM((blocks, up(len(pairs(history))), LANES), f32),
            dma((9,)),
            dma((9,)),
            dma((chunks, blocks)),
            dma((chunks, blocks)),
            dma((chunks,)),
            dma((chunks, blocks)),
            dma((chunks, blocks)),
            dma((chunks,)),
            dma((blocks,)),
            dma((blocks,)),
            dma((blocks,)),
            dma((blocks,)),
            dma((cells_x // LANES,)),
            dma,
            dma((3,)),
            dma((3,)),
            dma((cells_x // LANES,)),
        ],
        compiler_params=pltpu.CompilerParams(
            collective_id=0, has_side_effects=True, vmem_limit_bytes=60 * 2**20
        ),
        name="iterate",
    )(
        atom_table.reshape(5, rows),
        atom_counts,
        amps,
        widths,
        indirect.reshape(flat),
        past_indirect.reshape((history,) + flat),
        past_residual.reshape((history,) + flat),
        *tables,
    )
    return residual, earlier, mixing


def blend_kernel(mixing, indirect, residual, earlier, out, copied):
    history = earlier.shape[0]
    rows = indirect.shape[0]
    scale = [mixing[h, 0] for h in range(history + 1)]

    def step(group, carry):
        place = pl.ds(pl.multiple_of(group * SUB, SUB), SUB)
        last = residual[place, :]
        copied[place, :] = last
        mixed = scale[0] * (indirect[place, :] + MIX_STEP * last)
        for h in range(history):
            mixed = mixed + scale[h + 1] * earlier[h, place, :]
        out[place, :] = mixed
        return carry

    lax.fori_loop(0, rows // SUB, step, 0, unroll=4)


def blend(mixing, indirect, residual, earlier):
    history, rows, cells_x = earlier.shape
    tall = math.gcd(rows, 128)
    line = pl.BlockSpec((tall, cells_x), lambda c: (c, 0))
    stack = pl.BlockSpec((history, tall, cells_x), lambda c: (0, c, 0))
    return pl.pallas_call(
        blend_kernel,
        grid=(rows // tall,),
        in_specs=[pl.BlockSpec(memory_space=pltpu.SMEM), line, line, stack],
        out_specs=[line, line],
        out_shape=[jax.ShapeDtypeStruct((rows, cells_x), jnp.float32)] * 2,
        name="blend",
    )(mixing, indirect, residual, earlier)


def body(indirect, past_indirect, past_residual, atom_table, atom_counts, chi_amps, chi_widths):
    cells_y = indirect.shape[1]
    cells_z = indirect.shape[2]
    cells_x = indirect.shape[3]
    parts_y = lax.axis_size("gy")
    parts_z = lax.axis_size("gz")
    total_y = cells_y * parts_y
    total_z = cells_z * parts_z
    row_count = atom_table.shape[3]
    sizes = (
        parts_y, parts_z, indirect.shape[0], cells_y, cells_z, cells_x, past_residual.shape[0]
    )
    if fits(sizes, row_count):
        residual, earlier, mixing = iterate(
            sizes,
            indirect,
            past_indirect,
            past_residual,
            atom_table,
            atom_counts,
            chi_amps,
            chi_widths,
        )
        new_indirect, residual = blend(
            mixing, indirect.reshape(residual.shape), residual, earlier
        )
        return (new_indirect.reshape(indirect.shape), residual.reshape(indirect.shape))
    present = (lax.iota(jnp.int32, row_count) < atom_counts[0, 0]).astype(jnp.float32)
    bucket = jnp.concatenate([atom_table[0:3], atom_table[3:5] * present], 0)
    nearby = with_halo(bucket, (("gy", 1), ("gz", 2)), 1)
    nearby = nearby.reshape(5, 9 * row_count)
    potential_field = pencil_field(
        nearby,
        lax.axis_index("gy"),
        lax.axis_index("gz"),
        cells_y,
        cells_z,
        cells_x,
        total_y,
        total_z,
        float(SIGX),
    )
    potential_field = potential_field.reshape(2, cells_y, cells_z, cells_x)
    argument = indirect - potential_field
    closed = jnp.where(argument > 0, argument, jnp.expm1(jnp.minimum(argument, 0.0)))
    direct = closed - indirect
    table_x = hartley(cells_x)
    table_y = hartley(total_y)
    table_z = hartley(total_z)
    blocks = parts_y * parts_z
    width_x = cells_x // blocks
    grid_y = table_y.reshape(parts_y, cells_y, total_y)
    grid_z = table_z.reshape(parts_z, cells_z, total_z)
    outgoing = jnp.einsum(
        "scdx,xqk->qsdkc", direct, table_x.reshape(cells_x, blocks, width_x), precision=PRECISE
    )
    received = lax.all_to_all(outgoing, ("gy", "gz"), split_axis=0, concat_axis=0, tiled=True)
    wave_x = wave_squared(
        lax.axis_index(("gy", "gz")) * width_x + lax.iota(jnp.int32, width_x), cells_x
    )
    wave_square = (
        wave_x[:, None, None]
        + wave_squared(lax.iota(jnp.int32, total_z), total_z)[None, :, None]
        + wave_squared(lax.iota(jnp.int32, total_y), total_y)[None, None, :]
    )
    oxygen, mixed_site, hydrogen = lax.optimization_barrier(
        response(wave_square, chi_amps, chi_widths)
    )
    pieces = received.reshape(parts_y, parts_z, 2, cells_z, width_x, cells_y)
    partial_value = jnp.einsum("absdxc,acy->sbxdy", pieces, grid_y, precision=PRECISE)
    spectrum = jnp.einsum("sbxdy,bdz->sxzy", partial_value, grid_z, precision=PRECISE)
    coupled = jnp.stack(
        [
            oxygen * spectrum[0] + mixed_site * spectrum[1],
            mixed_site * spectrum[0] + hydrogen * spectrum[1],
        ]
    )
    partial_value = jnp.einsum("sxzy,bdz->sxbdy", coupled, grid_z, precision=PRECISE)
    returning = jnp.einsum("sxbdy,acy->absdxc", partial_value, grid_y, precision=PRECISE)
    returning = returning.reshape(blocks, 2, cells_z, width_x, cells_y)
    earlier = past_indirect + MIX_STEP * past_residual
    table_back = table_x.reshape(blocks, width_x, cells_x)
    received = lax.all_to_all(returning, ("gy", "gz"), split_axis=0, concat_axis=0, tiled=True)
    received, earlier = lax.optimization_barrier((received, earlier))
    total = jnp.einsum("qsdxc,qxk->sdck", received, table_back, precision=PRECISE)
    residual, products = finish(total, direct, indirect, past_residual)
    products = everywhere(jnp.sum(products, axis=(1, 2)), ("gy", "gz"))
    count = past_residual.shape[0] + 1
    where = {pair: n for n, pair in enumerate(pairs(count))}
    gram_matrix = jnp.stack(
        [products[where[min(i, j), max(i, j)]] for i in range(count) for j in range(count)]
    ).reshape(count, count)
    factor = jnp.linalg.cholesky(gram_matrix)
    weights = jax.scipy.linalg.cho_solve((factor, True), jnp.ones((count,), jnp.float32))
    mixing = weights / jnp.sum(weights)
    new_indirect = mix(mixing, indirect, residual, earlier)
    return (new_indirect, residual)


def solution(mesh):
    return jax.shard_map(
        body,
        mesh=mesh,
        in_specs=(
            P("groups", "gy", "gz", None),
            P("groups", None, "gy", "gz", None),
            P("groups", None, "gy", "gz", None),
            P("groups", "gy", "gz", None),
            P(("groups", "gy"), "gz"),
            P(),
            P(),
        ),
        out_specs=(P("groups", "gy", "gz", None), P("groups", "gy", "gz", None)),
        check_vma=False,
    )
```

```python
import functools
import math

import jax
import jax.numpy as jnp
import ml_dtypes
import numpy as np
from jax import lax
from jax.experimental import pallas as pl
from jax.experimental.pallas import tpu as pltpu
from jax.sharding import PartitionSpec as P

SIGX = 8


PRECISE = lax.Precision.HIGH
MIX_STEP = 0.3
BOND_OH = 1.9
BOND_HH = 3.1


def with_halo(cells, sides, width):
    for axis, dim in sides:
        count = lax.axis_size(axis)
        head = lax.slice_in_dim(cells, 0, width, axis=dim)
        tail = lax.slice_in_dim(cells, cells.shape[dim] - width, cells.shape[dim], axis=dim)
        cells = jnp.concatenate(
            [
                lax.ppermute(tail, axis, [(i, (i + 1) % count) for i in range(count)]),
                cells,
                lax.ppermute(head, axis, [((i + 1) % count, i) for i in range(count)]),
            ],
            axis=dim,
        )
    return cells


def hartley(length):
    position = lax.iota(jnp.int32, length)
    product = position[:, None] * position[None, :] % length
    angle = product.astype(jnp.float32) * (2.0 * math.pi / length)
    return (jnp.cos(angle) + jnp.sin(angle)) / math.sqrt(length)


def wave_squared(position, length):
    folded = jnp.where(2 * position > length, position - length, position)
    scaled = folded.astype(jnp.float32) * (2.0 * math.pi / length)
    return scaled * scaled


def response(wave_square, chi_amps, chi_widths):
    wavenumber = jnp.sqrt(wave_square)
    summed = [jnp.zeros_like(wave_square) for channel in range(3)]
    for which_term in range(chi_widths.shape[0]):
        gaussian_term = jnp.exp(-wave_square * (chi_widths[which_term] * chi_widths[which_term]))
        summed = [
            summed[channel] + chi_amps[channel, which_term] * gaussian_term for channel in range(3)
        ]
    oxygen = 1.0 + summed[0]
    mixed_site = 2.0 * jnp.sinc(wavenumber * (BOND_OH / math.pi)) + summed[1]
    hydrogen = 2.0 + 2.0 * jnp.sinc(wavenumber * (BOND_HH / math.pi)) + summed[2]
    return (oxygen, mixed_site, hydrogen)


def gaussian(offset, length, spread):
    offset = offset - length * jnp.floor(offset / length + 0.5)
    return jnp.exp(-0.5 * offset * offset / (spread * spread))


def pencil_field(
    atom_rows, pencil_y, pencil_z, cells_y, cells_z, total_x, total_y, total_z, spread_x
):
    cell_y = (pencil_y * cells_y + lax.iota(jnp.int32, cells_y)).astype(jnp.float32)
    cell_z = (pencil_z * cells_z + lax.iota(jnp.int32, cells_z)).astype(jnp.float32)
    cell_x = lax.iota(jnp.int32, total_x).astype(jnp.float32)
    along_y = gaussian(cell_y[:, None] - atom_rows[1][None, :], total_y, 0.5 * cells_y)
    along_z = gaussian(cell_z[:, None] - atom_rows[2][None, :], total_z, 0.5 * cells_z)
    along_x = gaussian(cell_x[:, None] - atom_rows[0][None, :], total_x, spread_x)
    left = atom_rows[3:5][:, None, None, :] * along_y[None, :, None, :] * along_z[None, None, :, :]
    left = left.reshape(2, cells_y * cells_z, atom_rows.shape[1])
    return jnp.einsum("sra,xa->srx", left, along_x, precision=PRECISE)


def pairs(count):
    return [(i, j) for i in range(count) for j in range(i, count)]


def everywhere(value, axes):
    for axis in axes:
        size = lax.axis_size(axis)
        if size & (size - 1):
            value = lax.psum(value, axis)
            continue
        step = 1
        while step < size:
            value = value + lax.ppermute(value, axis, [(i, i ^ step) for i in range(size)])
            step *= 2
    return value


def finish_kernel(total, direct, indirect, past, residual, products):
    history, _, rows, _, cells_x = past.shape
    couples = pairs(history + 1)

    @pl.when((pl.program_id(0) == 0) & (pl.program_id(1) == 0))
    def _():
        products[...] = jnp.zeros_like(products)

    lanes = products.shape[2]
    sums = tuple(products[n] for n in range(len(couples)))
    for lane in range(0, cells_x, lanes):
        columns = pl.ds(lane, lanes)

        def step(group, sums):
            first = pl.multiple_of(group * 8, 8)
            turned = jnp.swapaxes(total[0, :, pl.ds(first, 8), columns], 0, 1)
            for offset in range(8):
                row = first + offset
                now = turned[offset] - direct[0, row, :, columns] - indirect[0, row, :, columns]
                residual[0, row, :, columns] = now
                values = [now] + [past[h, 0, row, :, columns] for h in range(history)]
                sums = tuple(
                    sums[n] + values[i] * values[j] for n, (i, j) in enumerate(couples)
                )
            return sums

        sums = lax.fori_loop(0, rows // 8, step, sums)
    for n in range(len(couples)):
        products[n] = sums[n]


def block_rows(cells_y):
    return math.gcd(cells_y, 32)


def finish(total, direct, indirect, past_residual):
    history, sites, cells_y, cells_z, cells_x = past_residual.shape
    rows = block_rows(cells_y)
    field = pl.BlockSpec((1, rows, cells_z, cells_x), lambda s, c: (s, c, 0, 0))
    earlier = pl.BlockSpec((history, 1, rows, cells_z, cells_x), lambda s, c: (0, s, c, 0, 0))
    count = len(pairs(history + 1))
    lanes = min(cells_x, 128)
    return pl.pallas_call(
        finish_kernel,
        grid=(sites, cells_y // rows),
        in_specs=[
            pl.BlockSpec((1, cells_z, rows, cells_x), lambda s, c: (s, 0, c, 0)),
            field,
            field,
            earlier,
        ],
        out_specs=[field, pl.BlockSpec((count, cells_z, lanes), lambda s, c: (0, 0, 0))],
        out_shape=[
            jax.ShapeDtypeStruct(indirect.shape, jnp.float32),
            jax.ShapeDtypeStruct((count, cells_z, lanes), jnp.float32),
        ],
        name="finish",
    )(total, direct, indirect, past_residual)


def mix_kernel(mixing, indirect, residual, earlier, out):
    history = earlier.shape[0]
    rows = indirect.shape[1]
    scale = [mixing[h] for h in range(history + 1)]

    def step(row, carry):
        mixed = scale[0] * (indirect[0, row] + MIX_STEP * residual[0, row])
        for h in range(history):
            mixed = mixed + scale[h + 1] * earlier[h, 0, row]
        out[0, row] = mixed
        return carry

    lax.fori_loop(0, rows, step, 0, unroll=2)


def mix(mixing, indirect, residual, earlier):
    history, sites, cells_y, cells_z, cells_x = earlier.shape
    rows = block_rows(cells_y)
    field = pl.BlockSpec((1, rows, cells_z, cells_x), lambda s, c: (s, c, 0, 0))
    stack = pl.BlockSpec((history, 1, rows, cells_z, cells_x), lambda s, c: (0, s, c, 0, 0))
    return pl.pallas_call(
        mix_kernel,
        grid=(sites, cells_y // rows),
        in_specs=[pl.BlockSpec(memory_space=pltpu.SMEM), field, field, stack],
        out_specs=field,
        out_shape=jax.ShapeDtypeStruct(indirect.shape, jnp.float32),
        name="mix",
    )(mixing, indirect, residual, earlier)


def folded_angle(position, length):
    folded = jnp.where(2 * position > length, position - length, position)
    return folded.astype(jnp.float32) * (2.0 * math.pi / length)


def halves(value):
    high = value.astype(jnp.bfloat16)
    return high, (value - high.astype(jnp.float32)).astype(jnp.bfloat16)


def table_halves(table):
    high = table.astype(ml_dtypes.bfloat16)
    return high, (table - high.astype(np.float32)).astype(ml_dtypes.bfloat16)


def product(left, right, dims=(1, 0)):
    numbers = (((dims[0],), (dims[1],)), ((), ()))

    def dot(a, b):
        return lax.dot_general(a, b, numbers, preferred_element_type=jnp.float32)

    return dot(left[0], right[0]) + (dot(left[0], right[1]) + dot(left[1], right[0]))


def host_hartley(length):
    position = np.arange(length)
    angle = (position[:, None] * position[None, :] % length) * (2.0 * math.pi / length)
    return ((np.cos(angle) + np.sin(angle)) / math.sqrt(length)).astype(np.float32)


def sine_over(v):
    turns = jnp.floor(v * (1.0 / math.pi) + 0.5)
    r = (v - turns * 3.140625) - turns * (math.pi - 3.140625)
    odd = turns - 2.0 * jnp.floor(0.5 * turns)
    r2 = r * r
    series = -2.5052108e-08
    for term in (2.7557319e-06, -1.9841270e-04, 8.3333333e-03, -1.6666667e-01):
        series = series * r2 + term
    sine = (r + r * r2 * series) * (1.0 - 2.0 * odd)
    return jnp.where(v == 0.0, 1.0, sine / jnp.where(v == 0.0, 1.0, v))


def solve_ones(gram, count):
    rows = [[gram[min(i, j), max(i, j)] for j in range(count)] for i in range(count)]
    right = [jnp.ones_like(rows[0][0]) for i in range(count)]
    for k in range(count):
        inverse = 1.0 / rows[k][k]
        for i in range(k + 1, count):
            factor = rows[k][i] * inverse
            for j in range(i, count):
                rows[i][j] = rows[i][j] - factor * rows[k][j]
            right[i] = right[i] - factor * right[k]
    weights = [None] * count
    for k in reversed(range(count)):
        value = right[k]
        for j in range(k + 1, count):
            value = value - rows[k][j] * weights[j]
        weights[k] = value / rows[k][k]
    total = weights[0]
    for k in range(1, count):
        total = total + weights[k]
    return [weight / total for weight in weights]


SUB = 8
LANES = 128


def iterate_kernel(
    sizes,
    atoms,
    live,
    amps,
    widths,
    indirect,
    past_indirect,
    past_residual,
    table_wave,
    table_deep,
    mixing_out,
    earlier,
    field,
    near,
    wave,
    deep_wave,
    grid_x,
    grid_y,
    old,
    outgoing,
    planes,
    returned,
    total,
    spectrum,
    sums,
    sums_past,
    near_send,
    near_recv,
    go_send,
    go_recv,
    go_own,
    back_send,
    back_recv,
    back_own,
    last_send,
    last_recv,
    last_own,
    sum_send,
    sum_recv,
    past_send,
    past_recv,
    load_sem,
    table_sem,
    old_sem,
    earlier_sem,
):
    parts_y, parts_z, sites, cells_y, cells_z, cells_x, history = sizes
    total_y, total_z = parts_y * cells_y, parts_z * cells_z
    blocks = parts_y * parts_z
    chunks = cells_x // blocks // SUB
    lines = sites * cells_y
    strips = cells_x // LANES
    cells = lines * cells_z
    group = lax.axis_index("groups")
    my_y = lax.axis_index("gy")
    my_z = lax.axis_index("gz")
    me = my_y * parts_z + my_z

    def device(q):
        return (group, q // parts_z, q % parts_z)

    def remote(source, target, send, receive, q):
        return pltpu.make_async_remote_copy(
            src_ref=source,
            dst_ref=target,
            send_sem=send,
            recv_sem=receive,
            device_id=device(q),
            device_id_type=pl.DeviceIdType.MESH,
        )

    def each_partner(do):
        def step(i, carry):
            do((me + i) % blocks)
            return carry

        lax.fori_loop(1, blocks, step, 0)

    def strip(n):
        return slice(n * LANES, (n + 1) * LANES)

    loads = [
        pltpu.make_async_copy(indirect.at[:, strip(n)], field.at[n], load_sem.at[n])
        for n in range(strips)
    ]
    tables = [
        pltpu.make_async_copy(table_wave, wave, table_sem.at[0]),
        pltpu.make_async_copy(table_deep, deep_wave, table_sem.at[1]),
    ]
    for copy in loads + tables:
        copy.start()

    barrier = pltpu.get_barrier_semaphore()
    each_partner(
        lambda q: pl.semaphore_signal(
            barrier, inc=1, device_id=device(q), device_id_type=pl.DeviceIdType.MESH
        )
    )

    rows = atoms.shape[3]
    present = jnp.where(lax.broadcasted_iota(jnp.int32, (1, rows), 1) < live[0, 0], 1.0, 0.0)
    near[4] = jnp.zeros((SUB, rows), jnp.float32)
    for n in range(5):
        row = atoms[n, 0]
        near[4, n : n + 1, :] = row * present if n >= 3 else row
    pl.semaphore_wait(barrier, blocks - 1)

    shifts = [(a, b) for a in (-1, 0, 1) for b in (-1, 0, 1)]
    halo = []
    for n, (a, b) in enumerate(shifts):
        if (a, b) != (0, 0):
            q = ((my_y + a + parts_y) % parts_y) * parts_z + (my_z + b + parts_z) % parts_z
            slot = len(shifts) - 1 - n
            halo.append(
                remote(near.at[4], near.at[slot], near_send.at[n], near_recv.at[slot], q)
            )
            halo[-1].start()

    cell_x = lax.broadcasted_iota(jnp.int32, (cells_x, rows), 0).astype(jnp.float32)
    cell_y = (
        my_y * cells_y + lax.broadcasted_iota(jnp.int32, (cells_y, rows), 0)
    ).astype(jnp.float32)

    def spread_atoms(n):
        columns = slice(n * rows, (n + 1) * rows)
        along_x = gaussian(cell_x - near[n, 0:1, :], cells_x, float(SIGX))
        high, low = halves(along_x)
        grid_x[0, :, columns] = high
        grid_x[1, :, columns] = low
        grid_y[:, columns] = gaussian(cell_y - near[n, 1:2, :], total_y, 0.5 * cells_y)

    spread_atoms(4)
    for n in range(len(shifts)):
        if n != 4:
            remote(near.at[4], near.at[n], near_send.at[n], near_recv.at[n], me).wait_recv()
            spread_atoms(n)

    def old_loads(h, n):
        return (
            pltpu.make_async_copy(past_residual.at[h, :, strip(n)], old.at[h, n], old_sem.at[h, n]),
            pltpu.make_async_copy(
                past_indirect.at[h, :, strip(n)], earlier.at[h, n], earlier_sem.at[h, n]
            ),
        )

    for copy in loads + tables:
        copy.wait()
    for h in range(history):
        for n in range(strips):
            for copy in old_loads(h, n):
                copy.start()
    place_z = jnp.concatenate([near[n, 2:3, :] for n in range(len(shifts))], 1)
    strength = [
        jnp.concatenate([near[n, 3 + s : 4 + s, :] for n in range(len(shifts))], 1)
        for s in range(sites)
    ]

    def go(j, q):
        return remote(
            outgoing.at[j, q], planes.at[j, me], go_send.at[j, q], go_recv.at[j, me], q
        )

    def go_first(d, q):
        return remote(
            outgoing.at[0, q, d], planes.at[0, me, d], go_send.at[0, q], go_recv.at[0, me], q
        )

    def own(j):
        return pltpu.make_async_copy(outgoing.at[j, me], planes.at[j, me], go_own.at[j])

    def slab(d, carry):
        here_z = (my_z * cells_z + d).astype(jnp.float32)
        along_z = gaussian(here_z - place_z, total_z, 0.5 * cells_z)
        left = jnp.concatenate([grid_y[...] * (strength[s] * along_z) for s in range(sites)], 0)
        potential = product(halves(left), (grid_x[0], grid_x[1]), (1, 1))
        now = jnp.concatenate(
            [field[n, pl.ds(d, lines, stride=cells_z), :] for n in range(strips)], 1
        )
        argument = now - potential
        closed = jnp.where(argument > 0, argument, jnp.exp(jnp.minimum(argument, 0.0)) - 1.0)
        total[d] = -closed
        waves = product((wave[0], wave[1]), halves(closed - now), (1, 1))
        for s in range(sites):
            part = waves[:, s * cells_y : (s + 1) * cells_y]
            outgoing[:, :, d, s] = part.reshape(chunks, blocks, SUB, cells_y)
        each_partner(lambda q: go_first(d, q).start())
        return carry

    lax.fori_loop(0, cells_z, slab, 0)
    own(0).start()

    def issue(j, carry):
        own(j).start()
        each_partner(lambda q: go(j, q).start())
        return carry

    lax.fori_loop(1, chunks, issue, 0)

    for h in range(history):
        for n in range(strips):
            for copy in old_loads(h, n):
                copy.wait()
    couples = pairs(history)

    def stripe(t, acc):
        place = pl.ds(pl.multiple_of(t * SUB, SUB), SUB)
        acc = list(acc)
        for n in range(strips):
            values = [old[h, n, place, :] for h in range(history)]
            for h in range(history):
                earlier[h, n, place, :] = earlier[h, n, place, :] + MIX_STEP * values[h]
            for c, (i, j) in enumerate(couples):
                acc[c] = acc[c] + values[i] * values[j]
        return tuple(acc)

    zero = jnp.zeros((SUB, LANES), jnp.float32)
    acc = lax.fori_loop(0, cells // SUB, stripe, tuple(zero for _ in couples))

    def put(target, values):
        for n, value in enumerate(values):
            target[me, n : n + 1, :] = jnp.broadcast_to(jnp.sum(value).reshape(1, 1), (1, LANES))
        if len(values) < target.shape[1]:
            target[me, len(values) :, :] = jnp.zeros(
                (target.shape[1] - len(values), LANES), jnp.float32
            )

    put(sums_past, acc)

    def share_past(q):
        return remote(sums_past.at[me], sums_past.at[me], past_send.at[q], past_recv.at[me], q)

    each_partner(lambda q: share_past(q).start())

    def couple_step(t, j):
        tall_z = 4 * SUB
        first = pl.multiple_of(t * tall_z, tall_z)
        row = lax.broadcasted_iota(jnp.int32, (tall_z, total_y), 0)
        angle_z = folded_angle((first + row) // SUB, total_z)
        angle_x = folded_angle((j * blocks + me) * SUB + row % SUB, cells_x)
        angle_y = folded_angle(lax.broadcasted_iota(jnp.int32, (tall_z, total_y), 1), total_y)
        square = angle_x * angle_x + angle_z * angle_z + angle_y * angle_y
        number = jnp.sqrt(square)
        oxygen = jnp.ones_like(square)
        mixed = 2.0 * sine_over(number * BOND_OH)
        hydrogen = 2.0 + 2.0 * sine_over(number * BOND_HH)
        for term in range(widths.shape[0]):
            bell = jnp.exp(-square * (widths[term] * widths[term]))
            oxygen = oxygen + amps[0, term] * bell
            mixed = mixed + amps[1, term] * bell
            hydrogen = hydrogen + amps[2, term] * bell
        at = pl.ds(first, tall_z)
        first_site, second_site = spectrum[0, at, :], spectrum[1, at, :]
        spectrum[0, at, :] = oxygen * first_site + mixed * second_site
        spectrum[1, at, :] = mixed * first_site + hydrogen * second_site
        return j

    deep = total_z * SUB

    def middle(j):
        along_y = (wave[0], wave[1])
        along_z = (deep_wave[0], deep_wave[1])
        for s in range(sites):
            plane = jnp.concatenate(
                [
                    planes[j, a * parts_z : (a + 1) * parts_z, :, s].reshape(deep, cells_y)
                    for a in range(parts_y)
                ],
                1,
            )
            plane = product(halves(plane), along_y)
            spectrum[s] = product(along_z, halves(plane))
        lax.fori_loop(0, deep // (4 * SUB), couple_step, j)
        for s in range(sites):
            plane = product(along_z, halves(spectrum[s]))
            plane = product(halves(plane), along_y)
            for a in range(parts_y):
                part = plane[:, a * cells_y : (a + 1) * cells_y]
                planes[j, a * parts_z : (a + 1) * parts_z, :, s] = part.reshape(
                    parts_z, cells_z, SUB, cells_y
                )

    last = chunks - 1

    def back(j, q):
        return remote(
            planes.at[j, q], returned.at[j, me], back_send.at[j, q], back_recv.at[j, me], q
        )

    def back_self(j):
        return pltpu.make_async_copy(planes.at[j, me], returned.at[j, me], back_own.at[j])

    def back_last(d, q):
        return remote(
            planes.at[last, q, d],
            returned.at[last, me, d],
            last_send.at[d, q],
            last_recv.at[d, me],
            q,
        )

    def last_self(d):
        return pltpu.make_async_copy(
            planes.at[last, me, d], returned.at[last, me, d], last_own.at[d]
        )

    def middle_step(j, carry):
        own(j).wait()
        each_partner(
            lambda q: remote(
                outgoing.at[j, q], planes.at[j, q], go_send.at[j, q], go_recv.at[j, q], q
            ).wait_recv()
        )
        middle(j)

        @pl.when(j < last)
        def _():
            back_self(j).start()
            each_partner(lambda q: back(j, q).start())

        return carry

    lax.fori_loop(0, chunks, middle_step, 0)

    def send_last(d, carry):
        last_self(d).start()
        each_partner(lambda q: back_last(d, q).start())
        return carry

    lax.fori_loop(0, cells_z, send_last, 0)

    def lines_of(j, d):
        waves = jnp.concatenate(
            [returned[j, :, d, s].reshape(blocks * SUB, cells_y) for s in range(sites)], 1
        )
        here = pl.ds(pl.multiple_of(j * blocks * SUB, blocks * SUB), blocks * SUB)
        return product(halves(waves.T), (wave[0, here, :], wave[1, here, :]))

    def home(j, carry):
        back_self(j).wait()
        each_partner(
            lambda q: remote(
                planes.at[j, q], returned.at[j, q], back_send.at[j, q], back_recv.at[j, q], q
            ).wait_recv()
        )

        def slab_back(d, carry):
            total[d] = total[d] + lines_of(j, d)
            return carry

        return lax.fori_loop(0, cells_z, slab_back, carry)

    lax.fori_loop(0, last, home, 0)

    each_partner(
        lambda q: remote(
            sums_past.at[me], sums_past.at[q], past_send.at[q], past_recv.at[q], q
        ).wait_recv()
    )
    known = jnp.sum(sums_past[...], 0)

    def slab_last(d, acc):
        last_self(d).wait()
        each_partner(
            lambda q: remote(
                planes.at[last, q, d],
                returned.at[last, q, d],
                last_send.at[d, q],
                last_recv.at[d, q],
                q,
            ).wait_recv()
        )
        new = total[d] + lines_of(last, d)
        acc = list(acc)
        for n in range(strips):
            place = pl.ds(d, lines, stride=cells_z)
            now = new[:, strip(n)]
            field[n, place, :] = now
            for h in range(history + 1):
                both = now * (now if h == 0 else old[h - 1, n, place, :])
                acc[h] = acc[h] + jnp.sum(both.reshape(lines // SUB, SUB, LANES), 0)
        return tuple(acc)

    acc = lax.fori_loop(0, cells_z, slab_last, tuple(zero for _ in range(history + 1)))
    put(sums, acc)

    def share(q):
        return remote(sums.at[me], sums.at[me], sum_send.at[q], sum_recv.at[me], q)

    each_partner(lambda q: share(q).start())

    for copy in halo:
        copy.wait_send()

    def drain(q):
        share_past(q).wait_send()

        def step(j, carry):
            go(j, q).wait_send()

            @pl.when(j < last)
            def _():
                back(j, q).wait_send()

            return carry

        lax.fori_loop(0, chunks, step, 0)

        def step_last(d, carry):
            back_last(d, q).wait_send()
            return carry

        lax.fori_loop(0, cells_z, step_last, 0)

    each_partner(drain)
    each_partner(
        lambda q: remote(sums.at[me], sums.at[q], sum_send.at[q], sum_recv.at[q], q).wait_recv()
    )
    fresh = jnp.sum(sums[...], 0)
    gram = {(0, i): fresh[i : i + 1, :] for i in range(history + 1)}
    for n, (i, j) in enumerate(couples):
        gram[i + 1, j + 1] = known[n : n + 1, :]
    for n, value in enumerate(solve_ones(gram, history + 1)):
        mixing_out[n : n + 1, :] = value
    mixing_out[history + 1 :, :] = jnp.zeros(
        (mixing_out.shape[0] - history - 1, LANES), jnp.float32
    )
    each_partner(lambda q: share(q).wait_send())


def fits(sizes, rows):
    parts_y, parts_z, sites, cells_y, cells_z, cells_x, history = sizes
    blocks = parts_y * parts_z
    return (
        min(parts_y, parts_z) >= 3
        and sites == 2
        and cells_y == LANES
        and cells_z % SUB == 0
        and cells_x == parts_y * cells_y
        and cells_x % LANES == 0
        and cells_x % (blocks * SUB) == 0
        and rows % LANES == 0
        and history + 1 <= SUB
        and history * sites * cells_y * cells_z * cells_x * 4 <= 16 * 2**20
    )


def up(count):
    return -(-count // SUB) * SUB


def iterate(sizes, indirect, past_indirect, past_residual, atom_table, atom_counts, amps, widths):
    parts_y, parts_z, sites, cells_y, cells_z, cells_x, history = sizes
    total_y, total_z = parts_y * cells_y, parts_z * cells_z
    blocks = parts_y * parts_z
    chunks = cells_x // blocks // SUB
    rows = atom_table.shape[3]
    table_wave = np.stack(table_halves(host_hartley(cells_x)))
    table_deep = np.stack(
        table_halves(np.kron(host_hartley(total_z), np.eye(SUB, dtype=np.float32)))
    )
    flat = (sites * cells_y * cells_z, cells_x)
    strips = (cells_x // LANES, flat[0], LANES)
    block = (chunks, blocks, cells_z, sites, SUB, cells_y)
    anywhere = pl.BlockSpec(memory_space=pl.ANY)
    vector = pl.BlockSpec(memory_space=pltpu.VMEM)
    scalar = pl.BlockSpec(memory_space=pltpu.SMEM)
    dma = pltpu.SemaphoreType.DMA
    f32 = jnp.float32
    b16 = jnp.bfloat16
    return pl.pallas_call(
        functools.partial(iterate_kernel, sizes),
        in_specs=[vector, scalar, scalar, scalar] + [anywhere] * 5,
        out_specs=[vector] * 3,
        out_shape=[
            pltpu.VMEM((SUB, LANES), f32),
            pltpu.VMEM((history,) + strips, f32),
            pltpu.VMEM(strips, f32),
        ],
        scratch_shapes=[
            pltpu.VMEM((9, SUB, rows), f32),
            pltpu.VMEM(table_wave.shape, b16),
            pltpu.VMEM(table_deep.shape, b16),
            pltpu.VMEM((2, cells_x, 9 * rows), b16),
            pltpu.VMEM((cells_y, 9 * rows), f32),
            pltpu.VMEM((history,) + strips, f32),
            pltpu.VMEM(block, f32),
            pltpu.VMEM(block, f32),
            pltpu.VMEM(block, f32),
            pltpu.VMEM((cells_z, sites * cells_y, cells_x), f32),
            pltpu.VMEM((sites, total_z * SUB, total_y), f32),
            pltpu.VMEM((blocks, SUB, LANES), f32),
            pltpu.VMEM((blocks, up(len(pairs(history))), LANES), f32),
            dma((9,)),
            dma((9,)),
            dma((chunks, blocks)),
            dma((chunks, blocks)),
            dma((chunks,)),
            dma((chunks, blocks)),
            dma((chunks, blocks)),
            dma((chunks,)),
            dma((cells_z, blocks)),
            dma((cells_z, blocks)),
            dma((cells_z,)),
            dma((blocks,)),
            dma((blocks,)),
            dma((blocks,)),
            dma((blocks,)),
            dma((strips[0],)),
            dma((2,)),
            dma((history, strips[0])),
            dma((history, strips[0])),
        ],
        compiler_params=pltpu.CompilerParams(
            collective_id=0, has_side_effects=True, vmem_limit_bytes=43 * 2**20
        ),
        name="iterate",
    )(
        atom_table,
        atom_counts,
        amps,
        widths,
        indirect.reshape(flat),
        past_indirect.reshape((history,) + flat),
        past_residual.reshape((history,) + flat),
        jnp.asarray(table_wave),
        jnp.asarray(table_deep),
    )


BLEND_PARTS = 4


def blend_kernel(
    mixing, earlier, residual, indirect, new_out, residual_out, now, new, in_sem, out_sem, copy_sem
):
    history = earlier.shape[0]
    strips, cells, _ = residual.shape
    parts = in_sem.shape[0]
    tall = cells // parts

    def rows(p):
        return slice(p * tall, (p + 1) * tall)

    def strip(n):
        return slice(n * LANES, (n + 1) * LANES)

    loads = [
        [
            pltpu.make_async_copy(
                indirect.at[rows(p), strip(n)], now.at[n, rows(p)], in_sem.at[p, n]
            )
            for n in range(strips)
        ]
        for p in range(parts)
    ]
    stores = [
        [
            pltpu.make_async_copy(
                new.at[n, rows(p)], new_out.at[rows(p), strip(n)], out_sem.at[p, n]
            )
            for n in range(strips)
        ]
        for p in range(parts)
    ]
    copies = [
        pltpu.make_async_copy(residual.at[n], residual_out.at[:, strip(n)], copy_sem.at[n])
        for n in range(strips)
    ]
    for part in loads:
        for copy in part:
            copy.start()
    scale = [jnp.broadcast_to(mixing[h : h + 1, :], (SUB, LANES)) for h in range(history + 1)]
    for p in range(parts):
        for copy in loads[p]:
            copy.wait()

        def step(t, carry):
            place = pl.ds(pl.multiple_of(p * tall + t * SUB, SUB), SUB)
            for n in range(strips):
                mixed = scale[0] * (now[n, place, :] + MIX_STEP * residual[n, place, :])
                for h in range(history):
                    mixed = mixed + scale[h + 1] * earlier[h, n, place, :]
                new[n, place, :] = mixed
            return carry

        lax.fori_loop(0, tall // SUB, step, 0, unroll=2)
        for copy in stores[p]:
            copy.start()
        if p == 0:
            for copy in copies:
                copy.start()
    for part in stores + [copies]:
        for copy in part:
            copy.wait()


def blend(mixing, earlier, residual, indirect):
    strips, cells, _ = residual.shape
    flat = (cells, strips * LANES)
    parts = math.gcd(BLEND_PARTS, cells // SUB)
    anywhere = pl.BlockSpec(memory_space=pl.ANY)
    vector = pl.BlockSpec(memory_space=pltpu.VMEM)
    dma = pltpu.SemaphoreType.DMA
    held = [
        pltpu.with_memory_space_constraint(value, pltpu.VMEM)
        for value in (mixing, earlier, residual)
    ]
    outputs = pl.pallas_call(
        blend_kernel,
        in_specs=[vector] * 3 + [anywhere],
        out_specs=[anywhere] * 2,
        out_shape=[jax.ShapeDtypeStruct(flat, jnp.float32)] * 2,
        scratch_shapes=[
            pltpu.VMEM(residual.shape, jnp.float32),
            pltpu.VMEM(residual.shape, jnp.float32),
            dma((parts, strips)),
            dma((parts, strips)),
            dma((strips,)),
        ],
        compiler_params=pltpu.CompilerParams(vmem_limit_bytes=43 * 2**20),
        name="blend",
    )(*held, indirect.reshape(flat))
    return tuple(output.reshape(indirect.shape) for output in outputs)


def body(indirect, past_indirect, past_residual, atom_table, atom_counts, chi_amps, chi_widths):
    cells_y = indirect.shape[1]
    cells_z = indirect.shape[2]
    cells_x = indirect.shape[3]
    parts_y = lax.axis_size("gy")
    parts_z = lax.axis_size("gz")
    total_y = cells_y * parts_y
    total_z = cells_z * parts_z
    row_count = atom_table.shape[3]
    sizes = (
        parts_y, parts_z, indirect.shape[0], cells_y, cells_z, cells_x, past_residual.shape[0]
    )
    if fits(sizes, row_count):
        mixing, earlier, residual = iterate(
            sizes,
            indirect,
            past_indirect,
            past_residual,
            atom_table,
            atom_counts,
            chi_amps,
            chi_widths,
        )
        return blend(mixing, earlier, residual, indirect)
    present = (lax.iota(jnp.int32, row_count) < atom_counts[0, 0]).astype(jnp.float32)
    bucket = jnp.concatenate([atom_table[0:3], atom_table[3:5] * present], 0)
    nearby = with_halo(bucket, (("gy", 1), ("gz", 2)), 1)
    nearby = nearby.reshape(5, 9 * row_count)
    potential_field = pencil_field(
        nearby,
        lax.axis_index("gy"),
        lax.axis_index("gz"),
        cells_y,
        cells_z,
        cells_x,
        total_y,
        total_z,
        float(SIGX),
    )
    potential_field = potential_field.reshape(2, cells_y, cells_z, cells_x)
    argument = indirect - potential_field
    closed = jnp.where(argument > 0, argument, jnp.expm1(jnp.minimum(argument, 0.0)))
    direct = closed - indirect
    table_x = hartley(cells_x)
    table_y = hartley(total_y)
    table_z = hartley(total_z)
    blocks = parts_y * parts_z
    width_x = cells_x // blocks
    grid_y = table_y.reshape(parts_y, cells_y, total_y)
    grid_z = table_z.reshape(parts_z, cells_z, total_z)
    outgoing = jnp.einsum(
        "scdx,xqk->qsdkc", direct, table_x.reshape(cells_x, blocks, width_x), precision=PRECISE
    )
    received = lax.all_to_all(outgoing, ("gy", "gz"), split_axis=0, concat_axis=0, tiled=True)
    wave_x = wave_squared(
        lax.axis_index(("gy", "gz")) * width_x + lax.iota(jnp.int32, width_x), cells_x
    )
    wave_square = (
        wave_x[:, None, None]
        + wave_squared(lax.iota(jnp.int32, total_z), total_z)[None, :, None]
        + wave_squared(lax.iota(jnp.int32, total_y), total_y)[None, None, :]
    )
    oxygen, mixed_site, hydrogen = lax.optimization_barrier(
        response(wave_square, chi_amps, chi_widths)
    )
    pieces = received.reshape(parts_y, parts_z, 2, cells_z, width_x, cells_y)
    partial_value = jnp.einsum("absdxc,acy->sbxdy", pieces, grid_y, precision=PRECISE)
    spectrum = jnp.einsum("sbxdy,bdz->sxzy", partial_value, grid_z, precision=PRECISE)
    coupled = jnp.stack(
        [
            oxygen * spectrum[0] + mixed_site * spectrum[1],
            mixed_site * spectrum[0] + hydrogen * spectrum[1],
        ]
    )
    partial_value = jnp.einsum("sxzy,bdz->sxbdy", coupled, grid_z, precision=PRECISE)
    returning = jnp.einsum("sxbdy,acy->absdxc", partial_value, grid_y, precision=PRECISE)
    returning = returning.reshape(blocks, 2, cells_z, width_x, cells_y)
    earlier = past_indirect + MIX_STEP * past_residual
    table_back = table_x.reshape(blocks, width_x, cells_x)
    received = lax.all_to_all(returning, ("gy", "gz"), split_axis=0, concat_axis=0, tiled=True)
    received, earlier = lax.optimization_barrier((received, earlier))
    total = jnp.einsum("qsdxc,qxk->sdck", received, table_back, precision=PRECISE)
    residual, products = finish(total, direct, indirect, past_residual)
    products = everywhere(jnp.sum(products, axis=(1, 2)), ("gy", "gz"))
    count = past_residual.shape[0] + 1
    where = {pair: n for n, pair in enumerate(pairs(count))}
    gram_matrix = jnp.stack(
        [products[where[min(i, j), max(i, j)]] for i in range(count) for j in range(count)]
    ).reshape(count, count)
    factor = jnp.linalg.cholesky(gram_matrix)
    weights = jax.scipy.linalg.cho_solve((factor, True), jnp.ones((count,), jnp.float32))
    mixing = weights / jnp.sum(weights)
    new_indirect = mix(mixing, indirect, residual, earlier)
    return (new_indirect, residual)


def solution(mesh):
    return jax.shard_map(
        body,
        mesh=mesh,
        in_specs=(
            P("groups", "gy", "gz", None),
            P("groups", None, "gy", "gz", None),
            P("groups", None, "gy", "gz", None),
            P("groups", "gy", "gz", None),
            P(("groups", "gy"), "gz"),
            P(),
            P(),
        ),
        out_specs=(P("groups", "gy", "gz", None), P("groups", "gy", "gz", None)),
        check_vma=False,
    )
```

```python
import functools
import math

import jax
import jax.numpy as jnp
import ml_dtypes
import numpy as np
from jax import lax
from jax.experimental import pallas as pl
from jax.experimental.pallas import tpu as pltpu
from jax.sharding import PartitionSpec as P

SIGX = 8


PRECISE = lax.Precision.HIGH
MIX_STEP = 0.3
BOND_OH = 1.9
BOND_HH = 3.1


def with_halo(cells, sides, width):
    for axis, dim in sides:
        count = lax.axis_size(axis)
        head = lax.slice_in_dim(cells, 0, width, axis=dim)
        tail = lax.slice_in_dim(cells, cells.shape[dim] - width, cells.shape[dim], axis=dim)
        cells = jnp.concatenate(
            [
                lax.ppermute(tail, axis, [(i, (i + 1) % count) for i in range(count)]),
                cells,
                lax.ppermute(head, axis, [((i + 1) % count, i) for i in range(count)]),
            ],
            axis=dim,
        )
    return cells


def hartley(length):
    position = lax.iota(jnp.int32, length)
    product = position[:, None] * position[None, :] % length
    angle = product.astype(jnp.float32) * (2.0 * math.pi / length)
    return (jnp.cos(angle) + jnp.sin(angle)) / math.sqrt(length)


def wave_squared(position, length):
    folded = jnp.where(2 * position > length, position - length, position)
    scaled = folded.astype(jnp.float32) * (2.0 * math.pi / length)
    return scaled * scaled


def response(wave_square, chi_amps, chi_widths):
    wavenumber = jnp.sqrt(wave_square)
    summed = [jnp.zeros_like(wave_square) for channel in range(3)]
    for which_term in range(chi_widths.shape[0]):
        gaussian_term = jnp.exp(-wave_square * (chi_widths[which_term] * chi_widths[which_term]))
        summed = [
            summed[channel] + chi_amps[channel, which_term] * gaussian_term for channel in range(3)
        ]
    oxygen = 1.0 + summed[0]
    mixed_site = 2.0 * jnp.sinc(wavenumber * (BOND_OH / math.pi)) + summed[1]
    hydrogen = 2.0 + 2.0 * jnp.sinc(wavenumber * (BOND_HH / math.pi)) + summed[2]
    return (oxygen, mixed_site, hydrogen)


def gaussian(offset, length, spread):
    offset = offset - length * jnp.floor(offset / length + 0.5)
    return jnp.exp(-0.5 * offset * offset / (spread * spread))


def pencil_field(
    atom_rows, pencil_y, pencil_z, cells_y, cells_z, total_x, total_y, total_z, spread_x
):
    cell_y = (pencil_y * cells_y + lax.iota(jnp.int32, cells_y)).astype(jnp.float32)
    cell_z = (pencil_z * cells_z + lax.iota(jnp.int32, cells_z)).astype(jnp.float32)
    cell_x = lax.iota(jnp.int32, total_x).astype(jnp.float32)
    along_y = gaussian(cell_y[:, None] - atom_rows[1][None, :], total_y, 0.5 * cells_y)
    along_z = gaussian(cell_z[:, None] - atom_rows[2][None, :], total_z, 0.5 * cells_z)
    along_x = gaussian(cell_x[:, None] - atom_rows[0][None, :], total_x, spread_x)
    left = atom_rows[3:5][:, None, None, :] * along_y[None, :, None, :] * along_z[None, None, :, :]
    left = left.reshape(2, cells_y * cells_z, atom_rows.shape[1])
    return jnp.einsum("sra,xa->srx", left, along_x, precision=PRECISE)


def pairs(count):
    return [(i, j) for i in range(count) for j in range(i, count)]


def everywhere(value, axes):
    for axis in axes:
        size = lax.axis_size(axis)
        if size & (size - 1):
            value = lax.psum(value, axis)
            continue
        step = 1
        while step < size:
            value = value + lax.ppermute(value, axis, [(i, i ^ step) for i in range(size)])
            step *= 2
    return value


def finish_kernel(total, direct, indirect, past, residual, products):
    history, _, rows, _, cells_x = past.shape
    couples = pairs(history + 1)

    @pl.when((pl.program_id(0) == 0) & (pl.program_id(1) == 0))
    def _():
        products[...] = jnp.zeros_like(products)

    lanes = products.shape[2]
    sums = tuple(products[n] for n in range(len(couples)))
    for lane in range(0, cells_x, lanes):
        columns = pl.ds(lane, lanes)

        def step(group, sums):
            first = pl.multiple_of(group * 8, 8)
            turned = jnp.swapaxes(total[0, :, pl.ds(first, 8), columns], 0, 1)
            for offset in range(8):
                row = first + offset
                now = turned[offset] - direct[0, row, :, columns] - indirect[0, row, :, columns]
                residual[0, row, :, columns] = now
                values = [now] + [past[h, 0, row, :, columns] for h in range(history)]
                sums = tuple(
                    sums[n] + values[i] * values[j] for n, (i, j) in enumerate(couples)
                )
            return sums

        sums = lax.fori_loop(0, rows // 8, step, sums)
    for n in range(len(couples)):
        products[n] = sums[n]


def block_rows(cells_y):
    return math.gcd(cells_y, 32)


def finish(total, direct, indirect, past_residual):
    history, sites, cells_y, cells_z, cells_x = past_residual.shape
    rows = block_rows(cells_y)
    field = pl.BlockSpec((1, rows, cells_z, cells_x), lambda s, c: (s, c, 0, 0))
    earlier = pl.BlockSpec((history, 1, rows, cells_z, cells_x), lambda s, c: (0, s, c, 0, 0))
    count = len(pairs(history + 1))
    lanes = min(cells_x, 128)
    return pl.pallas_call(
        finish_kernel,
        grid=(sites, cells_y // rows),
        in_specs=[
            pl.BlockSpec((1, cells_z, rows, cells_x), lambda s, c: (s, 0, c, 0)),
            field,
            field,
            earlier,
        ],
        out_specs=[field, pl.BlockSpec((count, cells_z, lanes), lambda s, c: (0, 0, 0))],
        out_shape=[
            jax.ShapeDtypeStruct(indirect.shape, jnp.float32),
            jax.ShapeDtypeStruct((count, cells_z, lanes), jnp.float32),
        ],
        name="finish",
    )(total, direct, indirect, past_residual)


def mix_kernel(mixing, indirect, residual, earlier, out):
    history = earlier.shape[0]
    rows = indirect.shape[1]
    scale = [mixing[h] for h in range(history + 1)]

    def step(row, carry):
        mixed = scale[0] * (indirect[0, row] + MIX_STEP * residual[0, row])
        for h in range(history):
            mixed = mixed + scale[h + 1] * earlier[h, 0, row]
        out[0, row] = mixed
        return carry

    lax.fori_loop(0, rows, step, 0, unroll=2)


def mix(mixing, indirect, residual, earlier):
    history, sites, cells_y, cells_z, cells_x = earlier.shape
    rows = block_rows(cells_y)
    field = pl.BlockSpec((1, rows, cells_z, cells_x), lambda s, c: (s, c, 0, 0))
    stack = pl.BlockSpec((history, 1, rows, cells_z, cells_x), lambda s, c: (0, s, c, 0, 0))
    return pl.pallas_call(
        mix_kernel,
        grid=(sites, cells_y // rows),
        in_specs=[pl.BlockSpec(memory_space=pltpu.SMEM), field, field, stack],
        out_specs=field,
        out_shape=jax.ShapeDtypeStruct(indirect.shape, jnp.float32),
        name="mix",
    )(mixing, indirect, residual, earlier)


def folded_angle(position, length):
    folded = jnp.where(2 * position > length, position - length, position)
    return folded.astype(jnp.float32) * (2.0 * math.pi / length)


def halves(value):
    high = value.astype(jnp.bfloat16)
    return high, (value - high.astype(jnp.float32)).astype(jnp.bfloat16)


def table_halves(table):
    high = table.astype(ml_dtypes.bfloat16)
    return high, (table - high.astype(np.float32)).astype(ml_dtypes.bfloat16)


def product(left, right, dims=(1, 0)):
    numbers = (((dims[0],), (dims[1],)), ((), ()))

    def dot(a, b):
        return lax.dot_general(a, b, numbers, preferred_element_type=jnp.float32)

    return dot(left[0], right[0]) + (dot(left[0], right[1]) + dot(left[1], right[0]))


def host_hartley(length):
    position = np.arange(length)
    angle = (position[:, None] * position[None, :] % length) * (2.0 * math.pi / length)
    return ((np.cos(angle) + np.sin(angle)) / math.sqrt(length)).astype(np.float32)


def sine_over(v):
    turns = jnp.floor(v * (1.0 / math.pi) + 0.5)
    r = (v - turns * 3.140625) - turns * (math.pi - 3.140625)
    odd = turns - 2.0 * jnp.floor(0.5 * turns)
    r2 = r * r
    series = -2.5052108e-08
    for term in (2.7557319e-06, -1.9841270e-04, 8.3333333e-03, -1.6666667e-01):
        series = series * r2 + term
    sine = (r + r * r2 * series) * (1.0 - 2.0 * odd)
    return jnp.where(v == 0.0, 1.0, sine / jnp.where(v == 0.0, 1.0, v))


def solve_ones(gram, count):
    rows = [[gram[min(i, j), max(i, j)] for j in range(count)] for i in range(count)]
    right = [jnp.ones_like(rows[0][0]) for i in range(count)]
    for k in range(count):
        inverse = 1.0 / rows[k][k]
        for i in range(k + 1, count):
            factor = rows[k][i] * inverse
            for j in range(i, count):
                rows[i][j] = rows[i][j] - factor * rows[k][j]
            right[i] = right[i] - factor * right[k]
    weights = [None] * count
    for k in reversed(range(count)):
        value = right[k]
        for j in range(k + 1, count):
            value = value - rows[k][j] * weights[j]
        weights[k] = value / rows[k][k]
    total = weights[0]
    for k in range(1, count):
        total = total + weights[k]
    return [weight / total for weight in weights]


SUB = 8
LANES = 128


def bell(offset, length, spread):
    offset = offset - length * jnp.floor(offset * (1.0 / length) + 0.5)
    return jnp.exp(offset * offset * (-0.5 / (spread * spread)))


def iterate_kernel(
    sizes,
    atoms_in,
    live_in,
    amps_in,
    widths_in,
    indirect,
    past_indirect,
    past_residual,
    table_wave,
    table_deep,
    mixing_out,
    earlier,
    field,
    atoms,
    live,
    amps,
    widths,
    near,
    wave,
    deep_wave,
    grid_x,
    grid_y,
    old,
    outgoing,
    planes,
    returned,
    total,
    spectrum,
    sums,
    sums_past,
    small_sem,
    load_sem,
    near_sem,
    go_send,
    go_recv,
    back_send,
    back_recv,
    last_send,
    last_recv,
    sum_sem,
):
    parts_y, parts_z, sites, cells_y, cells_z, cells_x, history = sizes
    total_y, total_z = parts_y * cells_y, parts_z * cells_z
    blocks = parts_y * parts_z
    chunks = cells_x // blocks // SUB
    lines = sites * cells_y
    strips = cells_x // LANES
    cells = lines * cells_z
    group = lax.axis_index("groups")
    my_y = lax.axis_index("gy")
    my_z = lax.axis_index("gz")
    me = my_y * parts_z + my_z

    def device(q):
        return (group, q // parts_z, q % parts_z)

    def remote(source, target, send, receive, q):
        return pltpu.make_async_remote_copy(
            src_ref=source,
            dst_ref=target,
            send_sem=send,
            recv_sem=receive,
            device_id=device(q),
            device_id_type=pl.DeviceIdType.MESH,
        )

    def each_partner(do):
        def step(i, carry):
            do((me + i) % blocks)
            return carry

        lax.fori_loop(1, blocks, step, 0)

    def strip(n):
        return slice(n * LANES, (n + 1) * LANES)

    def taken(ref, sem):
        pltpu.make_async_copy(ref, ref, sem).wait()

    first = [
        pltpu.make_async_copy(atoms_in, atoms, small_sem.at[0]),
        pltpu.make_async_copy(live_in, live, small_sem.at[1]),
        pltpu.make_async_copy(amps_in, amps, small_sem.at[2]),
        pltpu.make_async_copy(widths_in, widths, small_sem.at[3]),
        pltpu.make_async_copy(table_wave, wave, small_sem.at[4]),
        pltpu.make_async_copy(table_deep, deep_wave, small_sem.at[5]),
    ]
    for copy in first:
        copy.start()
    for n in range(strips):
        pltpu.make_async_copy(indirect.at[:, strip(n)], field.at[n], load_sem.at[0]).start()

    barrier = pltpu.get_barrier_semaphore()
    each_partner(
        lambda q: pl.semaphore_signal(
            barrier, inc=1, device_id=device(q), device_id_type=pl.DeviceIdType.MESH
        )
    )

    rows = atoms.shape[3]
    for copy in first[:2]:
        copy.wait()
    present = jnp.where(lax.broadcasted_iota(jnp.int32, (1, rows), 1) < live[0, 0], 1.0, 0.0)
    near[4] = jnp.zeros((SUB, rows), jnp.float32)
    for n in range(5):
        row = atoms[n, 0]
        near[4, n : n + 1, :] = row * present if n >= 3 else row
    pl.semaphore_wait(barrier, blocks - 1)

    shifts = [(a, b) for a in (-1, 0, 1) for b in (-1, 0, 1)]
    for n, (a, b) in enumerate(shifts):
        if (a, b) != (0, 0):
            q = ((my_y + a + parts_y) % parts_y) * parts_z + (my_z + b + parts_z) % parts_z
            slot = len(shifts) - 1 - n
            remote(near.at[4], near.at[slot], near_sem.at[0], near_sem.at[1], q).start()

    cell_x = lax.broadcasted_iota(jnp.int32, (cells_x, rows), 0).astype(jnp.float32)
    cell_y = (
        my_y * cells_y + lax.broadcasted_iota(jnp.int32, (cells_y, rows), 0)
    ).astype(jnp.float32)

    def spread_atoms(n):
        columns = slice(n * rows, (n + 1) * rows)
        along_x = bell(cell_x - near[n, 0:1, :], cells_x, float(SIGX))
        high, low = halves(along_x)
        grid_x[0, :, columns] = high
        grid_x[1, :, columns] = low
        grid_y[:, columns] = bell(cell_y - near[n, 1:2, :], total_y, 0.5 * cells_y)

    spread_atoms(4)
    taken(near.at[0 : len(shifts) - 1], near_sem.at[1])
    for n in range(len(shifts)):
        if n != 4:
            spread_atoms(n)
    for copy in first[2:]:
        copy.wait()
    taken(field, load_sem.at[0])
    for h in range(history):
        for n in range(strips):
            pltpu.make_async_copy(
                past_residual.at[h, :, strip(n)], old.at[h, n], load_sem.at[1]
            ).start()
            pltpu.make_async_copy(
                past_indirect.at[h, :, strip(n)], earlier.at[h, n], load_sem.at[2]
            ).start()
    place_z = jnp.concatenate([near[n, 2:3, :] for n in range(len(shifts))], 1)
    strength = [
        jnp.concatenate([near[n, 3 + s : 4 + s, :] for n in range(len(shifts))], 1)
        for s in range(sites)
    ]

    def go(j, q):
        return remote(
            outgoing.at[j, q], planes.at[j, me], go_send.at[0], go_recv.at[j], q
        )

    def go_first(d, q):
        return remote(
            outgoing.at[0, q, d], planes.at[0, me, d], go_send.at[0], go_recv.at[0], q
        )

    def own(j):
        return pltpu.make_async_copy(outgoing.at[j, me], planes.at[j, me], go_recv.at[j])

    def slab(d, carry):
        here_z = (my_z * cells_z + d).astype(jnp.float32)
        along_z = bell(here_z - place_z, total_z, 0.5 * cells_z)
        left = jnp.concatenate([grid_y[...] * (strength[s] * along_z) for s in range(sites)], 0)
        potential = product(halves(left), (grid_x[0], grid_x[1]), (1, 1))
        now = jnp.concatenate(
            [field[n, pl.ds(d, lines, stride=cells_z), :] for n in range(strips)], 1
        )
        argument = now - potential
        closed = jnp.where(argument > 0, argument, jnp.exp(jnp.minimum(argument, 0.0)) - 1.0)
        total[d] = -closed
        waves = product((wave[0], wave[1]), halves(closed - now), (1, 1))
        for s in range(sites):
            part = waves[:, s * cells_y : (s + 1) * cells_y]
            outgoing[:, :, d, s] = part.reshape(chunks, blocks, SUB, cells_y)
        each_partner(lambda q: go_first(d, q).start())
        return carry

    lax.fori_loop(0, cells_z, slab, 0)
    own(0).start()

    def issue(j, carry):
        own(j).start()
        each_partner(lambda q: go(j, q).start())
        return carry

    lax.fori_loop(1, chunks, issue, 0)

    taken(old, load_sem.at[1])
    taken(earlier, load_sem.at[2])
    couples = pairs(history)

    def stripe(t, acc):
        place = pl.ds(pl.multiple_of(t * SUB, SUB), SUB)
        acc = list(acc)
        for n in range(strips):
            values = [old[h, n, place, :] for h in range(history)]
            for h in range(history):
                earlier[h, n, place, :] = earlier[h, n, place, :] + MIX_STEP * values[h]
            for c, (i, j) in enumerate(couples):
                acc[c] = acc[c] + values[i] * values[j]
        return tuple(acc)

    zero = jnp.zeros((SUB, LANES), jnp.float32)
    acc = lax.fori_loop(0, cells // SUB, stripe, tuple(zero for _ in couples))

    def put(target, values):
        target[me] = jnp.zeros(target.shape[1:], jnp.float32)
        for n, value in enumerate(values):
            target[me, n : n + 1, :] = jnp.sum(value, 0, keepdims=True)

    def share(tiles, which):
        each_partner(
            lambda q: remote(
                tiles.at[me], tiles.at[me], sum_sem.at[2 * which], sum_sem.at[2 * which + 1], q
            ).start()
        )

    def all_sums(tiles, which):
        taken(tiles.at[0 : blocks - 1], sum_sem.at[2 * which + 1])
        whole = jnp.sum(jnp.sum(tiles[...], 0), 1, keepdims=True)
        return jnp.broadcast_to(whole, tiles.shape[1:])

    put(sums_past, acc)
    share(sums_past, 0)

    def couple_step(t, j):
        tall_z = 4 * SUB
        first = pl.multiple_of(t * tall_z, tall_z)
        row = lax.broadcasted_iota(jnp.int32, (tall_z, total_y), 0)
        angle_z = folded_angle((first + row) // SUB, total_z)
        angle_x = folded_angle((j * blocks + me) * SUB + row % SUB, cells_x)
        angle_y = folded_angle(lax.broadcasted_iota(jnp.int32, (tall_z, total_y), 1), total_y)
        square = angle_x * angle_x + angle_z * angle_z + angle_y * angle_y
        number = jnp.sqrt(square)
        oxygen = jnp.ones_like(square)
        mixed = 2.0 * sine_over(number * BOND_OH)
        hydrogen = 2.0 + 2.0 * sine_over(number * BOND_HH)
        for term in range(widths.shape[0]):
            decay = jnp.exp(-square * (widths[term] * widths[term]))
            oxygen = oxygen + amps[0, term] * decay
            mixed = mixed + amps[1, term] * decay
            hydrogen = hydrogen + amps[2, term] * decay
        at = pl.ds(first, tall_z)
        first_site, second_site = spectrum[0, at, :], spectrum[1, at, :]
        spectrum[0, at, :] = oxygen * first_site + mixed * second_site
        spectrum[1, at, :] = mixed * first_site + hydrogen * second_site
        return j

    deep = total_z * SUB

    def middle(j):
        along_y = (wave[0], wave[1])
        along_z = (deep_wave[0], deep_wave[1])
        for s in range(sites):
            plane = jnp.concatenate(
                [
                    planes[j, a * parts_z : (a + 1) * parts_z, :, s].reshape(deep, cells_y)
                    for a in range(parts_y)
                ],
                1,
            )
            plane = product(halves(plane), along_y)
            spectrum[s] = product(along_z, halves(plane))
        lax.fori_loop(0, deep // (4 * SUB), couple_step, j)
        for s in range(sites):
            plane = product(along_z, halves(spectrum[s]))
            plane = product(halves(plane), along_y)
            for a in range(parts_y):
                part = plane[:, a * cells_y : (a + 1) * cells_y]
                planes[j, a * parts_z : (a + 1) * parts_z, :, s] = part.reshape(
                    parts_z, cells_z, SUB, cells_y
                )

    last = chunks - 1

    def back(j, q):
        return remote(
            planes.at[j, q], returned.at[j, me], back_send.at[0], back_recv.at[j], q
        )

    def back_self(j):
        return pltpu.make_async_copy(planes.at[j, me], returned.at[j, me], back_recv.at[j])

    def back_last(d, q):
        return remote(
            planes.at[last, q, d],
            returned.at[last, me, d],
            last_send.at[0],
            last_recv.at[d],
            q,
        )

    def last_self(d):
        return pltpu.make_async_copy(
            planes.at[last, me, d], returned.at[last, me, d], last_recv.at[d]
        )

    def middle_step(j, carry):
        taken(planes.at[j], go_recv.at[j])
        middle(j)

        @pl.when(j < last)
        def _():
            back_self(j).start()
            each_partner(lambda q: back(j, q).start())

        return carry

    lax.fori_loop(0, chunks, middle_step, 0)

    def send_last(d, carry):
        last_self(d).start()
        each_partner(lambda q: back_last(d, q).start())
        return carry

    lax.fori_loop(0, cells_z, send_last, 0)

    def lines_of(j, d):
        waves = jnp.concatenate(
            [returned[j, :, d, s].reshape(blocks * SUB, cells_y) for s in range(sites)], 1
        )
        here = pl.ds(pl.multiple_of(j * blocks * SUB, blocks * SUB), blocks * SUB)
        return product(halves(waves.T), (wave[0, here, :], wave[1, here, :]))

    def home(j, carry):
        taken(returned.at[j], back_recv.at[j])

        def slab_back(d, carry):
            total[d] = total[d] + lines_of(j, d)
            return carry

        return lax.fori_loop(0, cells_z, slab_back, carry)

    lax.fori_loop(0, last, home, 0)

    known = all_sums(sums_past, 0)
    taken(near.at[0 : len(shifts) - 1], near_sem.at[0])
    taken(sums_past.at[0 : blocks - 1], sum_sem.at[0])
    taken(outgoing.at[:, 0 : blocks - 1], go_send.at[0])
    taken(planes.at[0:last, 0 : blocks - 1], back_send.at[0])

    def slab_last(d, acc):
        taken(returned.at[last, :, d], last_recv.at[d])
        new = total[d] + lines_of(last, d)
        acc = list(acc)
        for n in range(strips):
            place = pl.ds(d, lines, stride=cells_z)
            now = new[:, strip(n)]
            field[n, place, :] = now
            for h in range(history + 1):
                both = now * (now if h == 0 else old[h - 1, n, place, :])
                acc[h] = acc[h] + jnp.sum(both.reshape(lines // SUB, SUB, LANES), 0)
        return tuple(acc)

    acc = lax.fori_loop(0, cells_z, slab_last, tuple(zero for _ in range(history + 1)))
    put(sums, acc)
    share(sums, 1)
    taken(planes.at[last, 0 : blocks - 1], last_send.at[0])
    fresh = all_sums(sums, 1)
    gram = {(0, i): fresh[i : i + 1, :] for i in range(history + 1)}
    for n, (i, j) in enumerate(couples):
        gram[i + 1, j + 1] = known[n : n + 1, :]
    for n, value in enumerate(solve_ones(gram, history + 1)):
        mixing_out[n : n + 1, :] = value
    mixing_out[history + 1 :, :] = jnp.zeros(
        (mixing_out.shape[0] - history - 1, LANES), jnp.float32
    )
    taken(sums.at[0 : blocks - 1], sum_sem.at[2])


def fits(sizes, rows):
    parts_y, parts_z, sites, cells_y, cells_z, cells_x, history = sizes
    blocks = parts_y * parts_z
    return (
        min(parts_y, parts_z) >= 3
        and sites == 2
        and cells_y == LANES
        and cells_z % SUB == 0
        and cells_x == parts_y * cells_y
        and cells_x % LANES == 0
        and cells_x % (blocks * SUB) == 0
        and rows % LANES == 0
        and history + 1 <= SUB
        and history * sites * cells_y * cells_z * cells_x * 4 <= 16 * 2**20
    )


def up(count):
    return -(-count // SUB) * SUB


def iterate(sizes, indirect, past_indirect, past_residual, atom_table, atom_counts, amps, widths):
    parts_y, parts_z, sites, cells_y, cells_z, cells_x, history = sizes
    total_y, total_z = parts_y * cells_y, parts_z * cells_z
    blocks = parts_y * parts_z
    chunks = cells_x // blocks // SUB
    rows = atom_table.shape[3]
    table_wave = np.stack(table_halves(host_hartley(cells_x)))
    table_deep = np.stack(
        table_halves(np.kron(host_hartley(total_z), np.eye(SUB, dtype=np.float32)))
    )
    flat = (sites * cells_y * cells_z, cells_x)
    strips = (cells_x // LANES, flat[0], LANES)
    block = (chunks, blocks, cells_z, sites, SUB, cells_y)
    anywhere = pl.BlockSpec(memory_space=pl.ANY)
    vector = pl.BlockSpec(memory_space=pltpu.VMEM)
    dma = pltpu.SemaphoreType.DMA
    f32 = jnp.float32
    b16 = jnp.bfloat16
    return pl.pallas_call(
        functools.partial(iterate_kernel, sizes),
        in_specs=[anywhere] * 9,
        out_specs=[vector] * 3,
        out_shape=[
            pltpu.VMEM((SUB, LANES), f32),
            pltpu.VMEM((history,) + strips, f32),
            pltpu.VMEM(strips, f32),
        ],
        scratch_shapes=[
            pltpu.VMEM(atom_table.shape, f32),
            pltpu.SMEM(atom_counts.shape, jnp.int32),
            pltpu.SMEM(amps.shape, f32),
            pltpu.SMEM(widths.shape, f32),
            pltpu.VMEM((9, SUB, rows), f32),
            pltpu.VMEM(table_wave.shape, b16),
            pltpu.VMEM(table_deep.shape, b16),
            pltpu.VMEM((2, cells_x, 9 * rows), b16),
            pltpu.VMEM((cells_y, 9 * rows), f32),
            pltpu.VMEM((history,) + strips, f32),
            pltpu.VMEM(block, f32),
            pltpu.VMEM(block, f32),
            pltpu.VMEM(block, f32),
            pltpu.VMEM((cells_z, sites * cells_y, cells_x), f32),
            pltpu.VMEM((sites, total_z * SUB, total_y), f32),
            pltpu.VMEM((blocks, SUB, LANES), f32),
            pltpu.VMEM((blocks, up(len(pairs(history))), LANES), f32),
            dma((6,)),
            dma((3,)),
            dma((2,)),
            dma((1,)),
            dma((chunks,)),
            dma((1,)),
            dma((chunks,)),
            dma((1,)),
            dma((cells_z,)),
            dma((4,)),
        ],
        compiler_params=pltpu.CompilerParams(
            collective_id=0, has_side_effects=True, vmem_limit_bytes=43 * 2**20
        ),
        name="iterate",
    )(
        atom_table,
        atom_counts,
        amps,
        widths,
        indirect.reshape(flat),
        past_indirect.reshape((history,) + flat),
        past_residual.reshape((history,) + flat),
        jnp.asarray(table_wave),
        jnp.asarray(table_deep),
    )


BLEND_PARTS = 4


def blend_kernel(
    mixing, earlier, residual, indirect, new_out, residual_out, now, new, in_sem, out_sem, copy_sem
):
    history = earlier.shape[0]
    strips, cells, _ = residual.shape
    parts = in_sem.shape[0]
    tall = cells // parts

    def rows(p):
        return slice(p * tall, (p + 1) * tall)

    def strip(n):
        return slice(n * LANES, (n + 1) * LANES)

    loads = [
        [
            pltpu.make_async_copy(
                indirect.at[rows(p), strip(n)], now.at[n, rows(p)], in_sem.at[p, n]
            )
            for n in range(strips)
        ]
        for p in range(parts)
    ]
    stores = [
        [
            pltpu.make_async_copy(
                new.at[n, rows(p)], new_out.at[rows(p), strip(n)], out_sem.at[p, n]
            )
            for n in range(strips)
        ]
        for p in range(parts)
    ]
    copies = [
        pltpu.make_async_copy(residual.at[n], residual_out.at[:, strip(n)], copy_sem.at[n])
        for n in range(strips)
    ]
    for part in loads:
        for copy in part:
            copy.start()
    for copy in copies:
        copy.start()
    scale = [jnp.broadcast_to(mixing[h : h + 1, :], (SUB, LANES)) for h in range(history + 1)]
    for p in range(parts):
        for copy in loads[p]:
            copy.wait()

        def step(t, carry):
            place = pl.ds(pl.multiple_of(p * tall + t * SUB, SUB), SUB)
            for n in range(strips):
                mixed = scale[0] * (now[n, place, :] + MIX_STEP * residual[n, place, :])
                for h in range(history):
                    mixed = mixed + scale[h + 1] * earlier[h, n, place, :]
                new[n, place, :] = mixed
            return carry

        lax.fori_loop(0, tall // SUB, step, 0, unroll=2)
        for copy in stores[p]:
            copy.start()
    for part in stores + [copies]:
        for copy in part:
            copy.wait()


def blend(mixing, earlier, residual, indirect):
    strips, cells, _ = residual.shape
    flat = (cells, strips * LANES)
    parts = math.gcd(BLEND_PARTS, cells // SUB)
    anywhere = pl.BlockSpec(memory_space=pl.ANY)
    vector = pl.BlockSpec(memory_space=pltpu.VMEM)
    dma = pltpu.SemaphoreType.DMA
    held = [
        pltpu.with_memory_space_constraint(value, pltpu.VMEM)
        for value in (mixing, earlier, residual)
    ]
    outputs = pl.pallas_call(
        blend_kernel,
        in_specs=[vector] * 3 + [anywhere],
        out_specs=[anywhere] * 2,
        out_shape=[jax.ShapeDtypeStruct(flat, jnp.float32)] * 2,
        scratch_shapes=[
            pltpu.VMEM(residual.shape, jnp.float32),
            pltpu.VMEM(residual.shape, jnp.float32),
            dma((parts, strips)),
            dma((parts, strips)),
            dma((strips,)),
        ],
        compiler_params=pltpu.CompilerParams(vmem_limit_bytes=43 * 2**20),
        name="blend",
    )(*held, indirect.reshape(flat))
    return tuple(output.reshape(indirect.shape) for output in outputs)


def body(indirect, past_indirect, past_residual, atom_table, atom_counts, chi_amps, chi_widths):
    cells_y = indirect.shape[1]
    cells_z = indirect.shape[2]
    cells_x = indirect.shape[3]
    parts_y = lax.axis_size("gy")
    parts_z = lax.axis_size("gz")
    total_y = cells_y * parts_y
    total_z = cells_z * parts_z
    row_count = atom_table.shape[3]
    sizes = (
        parts_y, parts_z, indirect.shape[0], cells_y, cells_z, cells_x, past_residual.shape[0]
    )
    if fits(sizes, row_count):
        mixing, earlier, residual = iterate(
            sizes,
            indirect,
            past_indirect,
            past_residual,
            atom_table,
            atom_counts,
            chi_amps,
            chi_widths,
        )
        return blend(mixing, earlier, residual, indirect)
    present = (lax.iota(jnp.int32, row_count) < atom_counts[0, 0]).astype(jnp.float32)
    bucket = jnp.concatenate([atom_table[0:3], atom_table[3:5] * present], 0)
    nearby = with_halo(bucket, (("gy", 1), ("gz", 2)), 1)
    nearby = nearby.reshape(5, 9 * row_count)
    potential_field = pencil_field(
        nearby,
        lax.axis_index("gy"),
        lax.axis_index("gz"),
        cells_y,
        cells_z,
        cells_x,
        total_y,
        total_z,
        float(SIGX),
    )
    potential_field = potential_field.reshape(2, cells_y, cells_z, cells_x)
    argument = indirect - potential_field
    closed = jnp.where(argument > 0, argument, jnp.expm1(jnp.minimum(argument, 0.0)))
    direct = closed - indirect
    table_x = hartley(cells_x)
    table_y = hartley(total_y)
    table_z = hartley(total_z)
    blocks = parts_y * parts_z
    width_x = cells_x // blocks
    grid_y = table_y.reshape(parts_y, cells_y, total_y)
    grid_z = table_z.reshape(parts_z, cells_z, total_z)
    outgoing = jnp.einsum(
        "scdx,xqk->qsdkc", direct, table_x.reshape(cells_x, blocks, width_x), precision=PRECISE
    )
    received = lax.all_to_all(outgoing, ("gy", "gz"), split_axis=0, concat_axis=0, tiled=True)
    wave_x = wave_squared(
        lax.axis_index(("gy", "gz")) * width_x + lax.iota(jnp.int32, width_x), cells_x
    )
    wave_square = (
        wave_x[:, None, None]
        + wave_squared(lax.iota(jnp.int32, total_z), total_z)[None, :, None]
        + wave_squared(lax.iota(jnp.int32, total_y), total_y)[None, None, :]
    )
    oxygen, mixed_site, hydrogen = lax.optimization_barrier(
        response(wave_square, chi_amps, chi_widths)
    )
    pieces = received.reshape(parts_y, parts_z, 2, cells_z, width_x, cells_y)
    partial_value = jnp.einsum("absdxc,acy->sbxdy", pieces, grid_y, precision=PRECISE)
    spectrum = jnp.einsum("sbxdy,bdz->sxzy", partial_value, grid_z, precision=PRECISE)
    coupled = jnp.stack(
        [
            oxygen * spectrum[0] + mixed_site * spectrum[1],
            mixed_site * spectrum[0] + hydrogen * spectrum[1],
        ]
    )
    partial_value = jnp.einsum("sxzy,bdz->sxbdy", coupled, grid_z, precision=PRECISE)
    returning = jnp.einsum("sxbdy,acy->absdxc", partial_value, grid_y, precision=PRECISE)
    returning = returning.reshape(blocks, 2, cells_z, width_x, cells_y)
    earlier = past_indirect + MIX_STEP * past_residual
    table_back = table_x.reshape(blocks, width_x, cells_x)
    received = lax.all_to_all(returning, ("gy", "gz"), split_axis=0, concat_axis=0, tiled=True)
    received, earlier = lax.optimization_barrier((received, earlier))
    total = jnp.einsum("qsdxc,qxk->sdck", received, table_back, precision=PRECISE)
    residual, products = finish(total, direct, indirect, past_residual)
    products = everywhere(jnp.sum(products, axis=(1, 2)), ("gy", "gz"))
    count = past_residual.shape[0] + 1
    where = {pair: n for n, pair in enumerate(pairs(count))}
    gram_matrix = jnp.stack(
        [products[where[min(i, j), max(i, j)]] for i in range(count) for j in range(count)]
    ).reshape(count, count)
    factor = jnp.linalg.cholesky(gram_matrix)
    weights = jax.scipy.linalg.cho_solve((factor, True), jnp.ones((count,), jnp.float32))
    mixing = weights / jnp.sum(weights)
    new_indirect = mix(mixing, indirect, residual, earlier)
    return (new_indirect, residual)


def solution(mesh):
    return jax.shard_map(
        body,
        mesh=mesh,
        in_specs=(
            P("groups", "gy", "gz", None),
            P("groups", None, "gy", "gz", None),
            P("groups", None, "gy", "gz", None),
            P("groups", "gy", "gz", None),
            P(("groups", "gy"), "gz"),
            P(),
            P(),
        ),
        out_specs=(P("groups", "gy", "gz", None), P("groups", "gy", "gz", None)),
        check_vma=False,
    )
```

```python
import functools
import math

import jax
import jax.numpy as jnp
import ml_dtypes
import numpy as np
from jax import lax
from jax.experimental import pallas as pl
from jax.experimental.pallas import tpu as pltpu
from jax.sharding import PartitionSpec as P

SIGX = 8


PRECISE = lax.Precision.HIGH
MIX_STEP = 0.3
BOND_OH = 1.9
BOND_HH = 3.1


def with_halo(cells, sides, width):
    for axis, dim in sides:
        count = lax.axis_size(axis)
        head = lax.slice_in_dim(cells, 0, width, axis=dim)
        tail = lax.slice_in_dim(cells, cells.shape[dim] - width, cells.shape[dim], axis=dim)
        cells = jnp.concatenate(
            [
                lax.ppermute(tail, axis, [(i, (i + 1) % count) for i in range(count)]),
                cells,
                lax.ppermute(head, axis, [((i + 1) % count, i) for i in range(count)]),
            ],
            axis=dim,
        )
    return cells


def hartley(length):
    position = lax.iota(jnp.int32, length)
    product = position[:, None] * position[None, :] % length
    angle = product.astype(jnp.float32) * (2.0 * math.pi / length)
    return (jnp.cos(angle) + jnp.sin(angle)) / math.sqrt(length)


def wave_squared(position, length):
    folded = jnp.where(2 * position > length, position - length, position)
    scaled = folded.astype(jnp.float32) * (2.0 * math.pi / length)
    return scaled * scaled


def response(wave_square, chi_amps, chi_widths):
    wavenumber = jnp.sqrt(wave_square)
    summed = [jnp.zeros_like(wave_square) for channel in range(3)]
    for which_term in range(chi_widths.shape[0]):
        gaussian_term = jnp.exp(-wave_square * (chi_widths[which_term] * chi_widths[which_term]))
        summed = [
            summed[channel] + chi_amps[channel, which_term] * gaussian_term for channel in range(3)
        ]
    oxygen = 1.0 + summed[0]
    mixed_site = 2.0 * jnp.sinc(wavenumber * (BOND_OH / math.pi)) + summed[1]
    hydrogen = 2.0 + 2.0 * jnp.sinc(wavenumber * (BOND_HH / math.pi)) + summed[2]
    return (oxygen, mixed_site, hydrogen)


def gaussian(offset, length, spread):
    offset = offset - length * jnp.floor(offset / length + 0.5)
    return jnp.exp(-0.5 * offset * offset / (spread * spread))


def pencil_field(
    atom_rows, pencil_y, pencil_z, cells_y, cells_z, total_x, total_y, total_z, spread_x
):
    cell_y = (pencil_y * cells_y + lax.iota(jnp.int32, cells_y)).astype(jnp.float32)
    cell_z = (pencil_z * cells_z + lax.iota(jnp.int32, cells_z)).astype(jnp.float32)
    cell_x = lax.iota(jnp.int32, total_x).astype(jnp.float32)
    along_y = gaussian(cell_y[:, None] - atom_rows[1][None, :], total_y, 0.5 * cells_y)
    along_z = gaussian(cell_z[:, None] - atom_rows[2][None, :], total_z, 0.5 * cells_z)
    along_x = gaussian(cell_x[:, None] - atom_rows[0][None, :], total_x, spread_x)
    left = atom_rows[3:5][:, None, None, :] * along_y[None, :, None, :] * along_z[None, None, :, :]
    left = left.reshape(2, cells_y * cells_z, atom_rows.shape[1])
    return jnp.einsum("sra,xa->srx", left, along_x, precision=PRECISE)


def pairs(count):
    return [(i, j) for i in range(count) for j in range(i, count)]


def everywhere(value, axes):
    for axis in axes:
        size = lax.axis_size(axis)
        if size & (size - 1):
            value = lax.psum(value, axis)
            continue
        step = 1
        while step < size:
            value = value + lax.ppermute(value, axis, [(i, i ^ step) for i in range(size)])
            step *= 2
    return value


def finish_kernel(total, direct, indirect, past, residual, products):
    history, _, rows, _, cells_x = past.shape
    couples = pairs(history + 1)

    @pl.when((pl.program_id(0) == 0) & (pl.program_id(1) == 0))
    def _():
        products[...] = jnp.zeros_like(products)

    lanes = products.shape[2]
    sums = tuple(products[n] for n in range(len(couples)))
    for lane in range(0, cells_x, lanes):
        columns = pl.ds(lane, lanes)

        def step(group, sums):
            first = pl.multiple_of(group * 8, 8)
            turned = jnp.swapaxes(total[0, :, pl.ds(first, 8), columns], 0, 1)
            for offset in range(8):
                row = first + offset
                now = turned[offset] - direct[0, row, :, columns] - indirect[0, row, :, columns]
                residual[0, row, :, columns] = now
                values = [now] + [past[h, 0, row, :, columns] for h in range(history)]
                sums = tuple(
                    sums[n] + values[i] * values[j] for n, (i, j) in enumerate(couples)
                )
            return sums

        sums = lax.fori_loop(0, rows // 8, step, sums)
    for n in range(len(couples)):
        products[n] = sums[n]


def block_rows(cells_y):
    return math.gcd(cells_y, 32)


def finish(total, direct, indirect, past_residual):
    history, sites, cells_y, cells_z, cells_x = past_residual.shape
    rows = block_rows(cells_y)
    field = pl.BlockSpec((1, rows, cells_z, cells_x), lambda s, c: (s, c, 0, 0))
    earlier = pl.BlockSpec((history, 1, rows, cells_z, cells_x), lambda s, c: (0, s, c, 0, 0))
    count = len(pairs(history + 1))
    lanes = min(cells_x, 128)
    return pl.pallas_call(
        finish_kernel,
        grid=(sites, cells_y // rows),
        in_specs=[
            pl.BlockSpec((1, cells_z, rows, cells_x), lambda s, c: (s, 0, c, 0)),
            field,
            field,
            earlier,
        ],
        out_specs=[field, pl.BlockSpec((count, cells_z, lanes), lambda s, c: (0, 0, 0))],
        out_shape=[
            jax.ShapeDtypeStruct(indirect.shape, jnp.float32),
            jax.ShapeDtypeStruct((count, cells_z, lanes), jnp.float32),
        ],
        name="finish",
    )(total, direct, indirect, past_residual)


def mix_kernel(mixing, indirect, residual, earlier, out):
    history = earlier.shape[0]
    rows = indirect.shape[1]
    scale = [mixing[h] for h in range(history + 1)]

    def step(row, carry):
        mixed = scale[0] * (indirect[0, row] + MIX_STEP * residual[0, row])
        for h in range(history):
            mixed = mixed + scale[h + 1] * earlier[h, 0, row]
        out[0, row] = mixed
        return carry

    lax.fori_loop(0, rows, step, 0, unroll=2)


def mix(mixing, indirect, residual, earlier):
    history, sites, cells_y, cells_z, cells_x = earlier.shape
    rows = block_rows(cells_y)
    field = pl.BlockSpec((1, rows, cells_z, cells_x), lambda s, c: (s, c, 0, 0))
    stack = pl.BlockSpec((history, 1, rows, cells_z, cells_x), lambda s, c: (0, s, c, 0, 0))
    return pl.pallas_call(
        mix_kernel,
        grid=(sites, cells_y // rows),
        in_specs=[pl.BlockSpec(memory_space=pltpu.SMEM), field, field, stack],
        out_specs=field,
        out_shape=jax.ShapeDtypeStruct(indirect.shape, jnp.float32),
        name="mix",
    )(mixing, indirect, residual, earlier)


def folded_angle(position, length):
    folded = jnp.where(2 * position > length, position - length, position)
    return folded.astype(jnp.float32) * (2.0 * math.pi / length)


def halves(value):
    high = value.astype(jnp.bfloat16)
    return high, (value - high.astype(jnp.float32)).astype(jnp.bfloat16)


def table_halves(table):
    high = table.astype(ml_dtypes.bfloat16)
    return high, (table - high.astype(np.float32)).astype(ml_dtypes.bfloat16)


def product(left, right, dims=(1, 0)):
    numbers = (((dims[0],), (dims[1],)), ((), ()))

    def dot(a, b):
        return lax.dot_general(a, b, numbers, preferred_element_type=jnp.float32)

    return dot(left[0], right[0]) + (dot(left[0], right[1]) + dot(left[1], right[0]))


def host_hartley(length):
    position = np.arange(length)
    angle = (position[:, None] * position[None, :] % length) * (2.0 * math.pi / length)
    return ((np.cos(angle) + np.sin(angle)) / math.sqrt(length)).astype(np.float32)


def sine_over(v):
    turns = jnp.floor(v * (1.0 / math.pi) + 0.5)
    r = (v - turns * 3.140625) - turns * (math.pi - 3.140625)
    odd = turns - 2.0 * jnp.floor(0.5 * turns)
    r2 = r * r
    series = -2.5052108e-08
    for term in (2.7557319e-06, -1.9841270e-04, 8.3333333e-03, -1.6666667e-01):
        series = series * r2 + term
    sine = (r + r * r2 * series) * (1.0 - 2.0 * odd)
    return jnp.where(v == 0.0, 1.0, sine / jnp.where(v == 0.0, 1.0, v))


def solve_ones(gram, count):
    rows = [[gram[min(i, j), max(i, j)] for j in range(count)] for i in range(count)]
    right = [jnp.ones_like(rows[0][0]) for i in range(count)]
    for k in range(count):
        inverse = 1.0 / rows[k][k]
        for i in range(k + 1, count):
            factor = rows[k][i] * inverse
            for j in range(i, count):
                rows[i][j] = rows[i][j] - factor * rows[k][j]
            right[i] = right[i] - factor * right[k]
    weights = [None] * count
    for k in reversed(range(count)):
        value = right[k]
        for j in range(k + 1, count):
            value = value - rows[k][j] * weights[j]
        weights[k] = value / rows[k][k]
    total = weights[0]
    for k in range(1, count):
        total = total + weights[k]
    return [weight / total for weight in weights]


SUB = 8
LANES = 128


def bell(offset, length, spread):
    offset = offset - length * jnp.floor(offset * (1.0 / length) + 0.5)
    return jnp.exp(offset * offset * (-0.5 / (spread * spread)))


def iterate_kernel(
    sizes,
    atoms_in,
    live_in,
    amps_in,
    widths_in,
    indirect,
    indirect_tiles,
    past_indirect,
    past_residual,
    table_wave,
    table_deep,
    mixing_out,
    earlier,
    field,
    outgoing,
    atoms,
    live,
    amps,
    widths,
    near,
    wave,
    deep_wave,
    grid_x,
    grid_y,
    old,
    planes,
    returned,
    total,
    spectrum,
    sums,
    sums_past,
    small_sem,
    load_sem,
    near_sem,
    go_send,
    go_recv,
    back_send,
    back_recv,
    last_send,
    last_recv,
    sum_sem,
):
    parts_y, parts_z, sites, cells_y, cells_z, cells_x, history = sizes
    total_y, total_z = parts_y * cells_y, parts_z * cells_z
    blocks = parts_y * parts_z
    chunks = cells_x // blocks // SUB
    lines = sites * cells_y
    strips = cells_x // LANES
    cells = lines * cells_z
    group = lax.axis_index("groups")
    my_y = lax.axis_index("gy")
    my_z = lax.axis_index("gz")
    me = my_y * parts_z + my_z

    def device(q):
        return (group, q // parts_z, q % parts_z)

    def remote(source, target, send, receive, q):
        return pltpu.make_async_remote_copy(
            src_ref=source,
            dst_ref=target,
            send_sem=send,
            recv_sem=receive,
            device_id=device(q),
            device_id_type=pl.DeviceIdType.MESH,
        )

    def each_partner(do):
        def step(i, carry):
            do((me + i) % blocks)
            return carry

        lax.fori_loop(1, blocks, step, 0)

    def strip(n):
        return slice(n * LANES, (n + 1) * LANES)

    def taken(ref, sem):
        pltpu.make_async_copy(ref, ref, sem).wait()

    first = [
        pltpu.make_async_copy(atoms_in, atoms, small_sem.at[0]),
        pltpu.make_async_copy(live_in, live, small_sem.at[1]),
        pltpu.make_async_copy(amps_in, amps, small_sem.at[2]),
        pltpu.make_async_copy(widths_in, widths, small_sem.at[3]),
        pltpu.make_async_copy(table_wave, wave, small_sem.at[4]),
        pltpu.make_async_copy(table_deep, deep_wave, small_sem.at[5]),
    ]
    for copy in first:
        copy.start()
    for n in range(strips):
        pltpu.make_async_copy(indirect.at[:, strip(n)], field.at[n], load_sem.at[0]).start()

    barrier = pltpu.get_barrier_semaphore()
    each_partner(
        lambda q: pl.semaphore_signal(
            barrier, inc=1, device_id=device(q), device_id_type=pl.DeviceIdType.MESH
        )
    )

    rows = atoms.shape[3]
    for copy in first[:2]:
        copy.wait()
    present = jnp.where(lax.broadcasted_iota(jnp.int32, (1, rows), 1) < live[0, 0], 1.0, 0.0)
    near[4] = jnp.zeros((SUB, rows), jnp.float32)
    for n in range(5):
        row = atoms[n, 0]
        near[4, n : n + 1, :] = row * present if n >= 3 else row
    pl.semaphore_wait(barrier, blocks - 1)

    shifts = [(a, b) for a in (-1, 0, 1) for b in (-1, 0, 1)]
    for n, (a, b) in enumerate(shifts):
        if (a, b) != (0, 0):
            q = ((my_y + a + parts_y) % parts_y) * parts_z + (my_z + b + parts_z) % parts_z
            slot = len(shifts) - 1 - n
            remote(near.at[4], near.at[slot], near_sem.at[0], near_sem.at[1], q).start()

    cell_x = lax.broadcasted_iota(jnp.int32, (cells_x, rows), 0).astype(jnp.float32)
    cell_y = (
        my_y * cells_y + lax.broadcasted_iota(jnp.int32, (cells_y, rows), 0)
    ).astype(jnp.float32)

    def spread_atoms(n):
        columns = slice(n * rows, (n + 1) * rows)
        along_x = bell(cell_x - near[n, 0:1, :], cells_x, float(SIGX))
        high, low = halves(along_x)
        grid_x[0, :, columns] = high
        grid_x[1, :, columns] = low
        grid_y[:, columns] = bell(cell_y - near[n, 1:2, :], total_y, 0.5 * cells_y)

    spread_atoms(4)
    taken(near.at[0 : len(shifts) - 1], near_sem.at[1])
    for n in range(len(shifts)):
        if n != 4:
            spread_atoms(n)
    for copy in first[2:]:
        copy.wait()
    taken(field, load_sem.at[0])
    for h in range(history):
        for n in range(strips):
            pltpu.make_async_copy(
                past_residual.at[h, :, strip(n)], old.at[h, n], load_sem.at[1]
            ).start()
            pltpu.make_async_copy(
                past_indirect.at[h, :, strip(n)], earlier.at[h, n], load_sem.at[2]
            ).start()
    place_z = jnp.concatenate([near[n, 2:3, :] for n in range(len(shifts))], 1)
    strength = [
        jnp.concatenate([near[n, 3 + s : 4 + s, :] for n in range(len(shifts))], 1)
        for s in range(sites)
    ]

    def go(j, q):
        return remote(
            outgoing.at[j, q], planes.at[j, me], go_send.at[0], go_recv.at[j], q
        )

    def go_first(d, q):
        return remote(
            outgoing.at[0, q, d], planes.at[0, me, d], go_send.at[0], go_recv.at[0], q
        )

    def own(j):
        return pltpu.make_async_copy(outgoing.at[j, me], planes.at[j, me], go_recv.at[j])

    def slab(d, carry):
        here_z = (my_z * cells_z + d).astype(jnp.float32)
        along_z = bell(here_z - place_z, total_z, 0.5 * cells_z)
        left = jnp.concatenate([grid_y[...] * (strength[s] * along_z) for s in range(sites)], 0)
        potential = product(halves(left), (grid_x[0], grid_x[1]), (1, 1))
        now = jnp.concatenate(
            [field[n, pl.ds(d, lines, stride=cells_z), :] for n in range(strips)], 1
        )
        argument = now - potential
        closed = jnp.where(argument > 0, argument, jnp.exp(jnp.minimum(argument, 0.0)) - 1.0)
        total[d] = -closed
        waves = product((wave[0], wave[1]), halves(closed - now), (1, 1))
        for s in range(sites):
            part = waves[:, s * cells_y : (s + 1) * cells_y]
            outgoing[:, :, d, s] = part.reshape(chunks, blocks, SUB, cells_y)
        each_partner(lambda q: go_first(d, q).start())
        return carry

    lax.fori_loop(0, cells_z, slab, 0)
    own(0).start()

    def issue(j, carry):
        own(j).start()
        each_partner(lambda q: go(j, q).start())
        return carry

    lax.fori_loop(1, chunks, issue, 0)

    taken(old, load_sem.at[1])
    taken(earlier, load_sem.at[2])
    couples = pairs(history)

    def stripe(t, acc):
        place = pl.ds(pl.multiple_of(t * SUB, SUB), SUB)
        acc = list(acc)
        for n in range(strips):
            values = [old[h, n, place, :] for h in range(history)]
            for h in range(history):
                earlier[h, n, place, :] = earlier[h, n, place, :] + MIX_STEP * values[h]
            for c, (i, j) in enumerate(couples):
                acc[c] = acc[c] + values[i] * values[j]
        return tuple(acc)

    zero = jnp.zeros((SUB, LANES), jnp.float32)
    acc = lax.fori_loop(0, cells // SUB, stripe, tuple(zero for _ in couples))

    def put(target, values):
        target[me] = jnp.zeros(target.shape[1:], jnp.float32)
        for n, value in enumerate(values):
            target[me, n : n + 1, :] = jnp.sum(value, 0, keepdims=True)

    def share(tiles, which):
        each_partner(
            lambda q: remote(
                tiles.at[me], tiles.at[me], sum_sem.at[2 * which], sum_sem.at[2 * which + 1], q
            ).start()
        )

    def all_sums(tiles, which):
        taken(tiles.at[0 : blocks - 1], sum_sem.at[2 * which + 1])
        whole = jnp.sum(jnp.sum(tiles[...], 0), 1, keepdims=True)
        return jnp.broadcast_to(whole, tiles.shape[1:])

    put(sums_past, acc)
    share(sums_past, 0)

    def couple_step(t, j):
        tall_z = 4 * SUB
        first = pl.multiple_of(t * tall_z, tall_z)
        row = lax.broadcasted_iota(jnp.int32, (tall_z, total_y), 0)
        angle_z = folded_angle((first + row) // SUB, total_z)
        angle_x = folded_angle((j * blocks + me) * SUB + row % SUB, cells_x)
        angle_y = folded_angle(lax.broadcasted_iota(jnp.int32, (tall_z, total_y), 1), total_y)
        square = angle_x * angle_x + angle_z * angle_z + angle_y * angle_y
        number = jnp.sqrt(square)
        oxygen = jnp.ones_like(square)
        mixed = 2.0 * sine_over(number * BOND_OH)
        hydrogen = 2.0 + 2.0 * sine_over(number * BOND_HH)
        for term in range(widths.shape[0]):
            decay = jnp.exp(-square * (widths[term] * widths[term]))
            oxygen = oxygen + amps[0, term] * decay
            mixed = mixed + amps[1, term] * decay
            hydrogen = hydrogen + amps[2, term] * decay
        at = pl.ds(first, tall_z)
        first_site, second_site = spectrum[0, at, :], spectrum[1, at, :]
        spectrum[0, at, :] = oxygen * first_site + mixed * second_site
        spectrum[1, at, :] = mixed * first_site + hydrogen * second_site
        return j

    deep = total_z * SUB

    def middle(j):
        along_y = (wave[0], wave[1])
        along_z = (deep_wave[0], deep_wave[1])
        for s in range(sites):
            plane = jnp.concatenate(
                [
                    planes[j, a * parts_z : (a + 1) * parts_z, :, s].reshape(deep, cells_y)
                    for a in range(parts_y)
                ],
                1,
            )
            plane = product(halves(plane), along_y)
            spectrum[s] = product(along_z, halves(plane))
        lax.fori_loop(0, deep // (4 * SUB), couple_step, j)
        for s in range(sites):
            plane = product(along_z, halves(spectrum[s]))
            plane = product(halves(plane), along_y)
            for a in range(parts_y):
                part = plane[:, a * cells_y : (a + 1) * cells_y]
                planes[j, a * parts_z : (a + 1) * parts_z, :, s] = part.reshape(
                    parts_z, cells_z, SUB, cells_y
                )

    last = chunks - 1

    def back(j, q):
        return remote(
            planes.at[j, q], returned.at[j, me], back_send.at[0], back_recv.at[j], q
        )

    def back_self(j):
        return pltpu.make_async_copy(planes.at[j, me], returned.at[j, me], back_recv.at[j])

    def back_last(d, q):
        return remote(
            planes.at[last, q, d],
            returned.at[last, me, d],
            last_send.at[0],
            last_recv.at[d],
            q,
        )

    def last_self(d):
        return pltpu.make_async_copy(
            planes.at[last, me, d], returned.at[last, me, d], last_recv.at[d]
        )

    def middle_step(j, carry):
        taken(planes.at[j], go_recv.at[j])
        middle(j)

        @pl.when(j < last)
        def _():
            back_self(j).start()
            each_partner(lambda q: back(j, q).start())

        return carry

    lax.fori_loop(0, chunks, middle_step, 0)

    def send_last(d, carry):
        last_self(d).start()
        each_partner(lambda q: back_last(d, q).start())
        return carry

    lax.fori_loop(0, cells_z, send_last, 0)

    def lines_of(j, d):
        waves = jnp.concatenate(
            [returned[j, :, d, s].reshape(blocks * SUB, cells_y) for s in range(sites)], 1
        )
        here = pl.ds(pl.multiple_of(j * blocks * SUB, blocks * SUB), blocks * SUB)
        return product(halves(waves.T), (wave[0, here, :], wave[1, here, :]))

    def home(j, carry):
        taken(returned.at[j], back_recv.at[j])

        def slab_back(d, carry):
            total[d] = total[d] + lines_of(j, d)
            return carry

        return lax.fori_loop(0, cells_z, slab_back, carry)

    lax.fori_loop(0, last, home, 0)

    known = all_sums(sums_past, 0)
    taken(near.at[0 : len(shifts) - 1], near_sem.at[0])
    taken(sums_past.at[0 : blocks - 1], sum_sem.at[0])
    taken(outgoing.at[:, 0 : blocks - 1], go_send.at[0])
    taken(planes.at[0:last, 0 : blocks - 1], back_send.at[0])
    again = [
        pltpu.make_async_copy(
            indirect_tiles.at[:, :, :, :, strip(n)], outgoing.at[n], load_sem.at[3 + n]
        )
        for n in range(strips)
    ]
    for copy in again:
        copy.start()

    def slab_last(d, acc):
        taken(returned.at[last, :, d], last_recv.at[d])
        new = total[d] + lines_of(last, d)
        acc = list(acc)
        for n in range(strips):
            place = pl.ds(d, lines, stride=cells_z)
            now = new[:, strip(n)]
            field[n, place, :] = now
            for h in range(history + 1):
                both = now * (now if h == 0 else old[h - 1, n, place, :])
                acc[h] = acc[h] + jnp.sum(both.reshape(lines // SUB, SUB, LANES), 0)
        return tuple(acc)

    acc = lax.fori_loop(0, cells_z, slab_last, tuple(zero for _ in range(history + 1)))
    put(sums, acc)
    share(sums, 1)
    taken(planes.at[last, 0 : blocks - 1], last_send.at[0])
    fresh = all_sums(sums, 1)
    gram = {(0, i): fresh[i : i + 1, :] for i in range(history + 1)}
    for n, (i, j) in enumerate(couples):
        gram[i + 1, j + 1] = known[n : n + 1, :]
    for n, value in enumerate(solve_ones(gram, history + 1)):
        mixing_out[n : n + 1, :] = value
    mixing_out[history + 1 :, :] = jnp.zeros(
        (mixing_out.shape[0] - history - 1, LANES), jnp.float32
    )
    taken(sums.at[0 : blocks - 1], sum_sem.at[2])
    for copy in again:
        copy.wait()


def fits(sizes, rows):
    parts_y, parts_z, sites, cells_y, cells_z, cells_x, history = sizes
    blocks = parts_y * parts_z
    return (
        min(parts_y, parts_z) >= 3
        and sites == 2
        and cells_y == LANES
        and cells_z % SUB == 0
        and cells_x == parts_y * cells_y
        and cells_x % LANES == 0
        and blocks * SUB == LANES
        and rows % LANES == 0
        and history + 1 <= SUB
        and history * sites * cells_y * cells_z * cells_x * 4 <= 16 * 2**20
    )


def up(count):
    return -(-count // SUB) * SUB


def iterate(sizes, indirect, past_indirect, past_residual, atom_table, atom_counts, amps, widths):
    parts_y, parts_z, sites, cells_y, cells_z, cells_x, history = sizes
    total_y, total_z = parts_y * cells_y, parts_z * cells_z
    blocks = parts_y * parts_z
    chunks = cells_x // blocks // SUB
    rows = atom_table.shape[3]
    table_wave = np.stack(table_halves(host_hartley(cells_x)))
    table_deep = np.stack(
        table_halves(np.kron(host_hartley(total_z), np.eye(SUB, dtype=np.float32)))
    )
    flat = (sites * cells_y * cells_z, cells_x)
    strips = (cells_x // LANES, flat[0], LANES)
    block = (chunks, blocks, cells_z, sites, SUB, cells_y)
    anywhere = pl.BlockSpec(memory_space=pl.ANY)
    vector = pl.BlockSpec(memory_space=pltpu.VMEM)
    dma = pltpu.SemaphoreType.DMA
    f32 = jnp.float32
    b16 = jnp.bfloat16
    return pl.pallas_call(
        functools.partial(iterate_kernel, sizes),
        in_specs=[anywhere] * 10,
        out_specs=[vector] * 4,
        out_shape=[
            pltpu.VMEM((SUB, LANES), f32),
            pltpu.VMEM((history,) + strips, f32),
            pltpu.VMEM(strips, f32),
            pltpu.VMEM(block, f32),
        ],
        scratch_shapes=[
            pltpu.VMEM(atom_table.shape, f32),
            pltpu.SMEM(atom_counts.shape, jnp.int32),
            pltpu.SMEM(amps.shape, f32),
            pltpu.SMEM(widths.shape, f32),
            pltpu.VMEM((9, SUB, rows), f32),
            pltpu.VMEM(table_wave.shape, b16),
            pltpu.VMEM(table_deep.shape, b16),
            pltpu.VMEM((2, cells_x, 9 * rows), b16),
            pltpu.VMEM((cells_y, 9 * rows), f32),
            pltpu.VMEM((history,) + strips, f32),
            pltpu.VMEM(block, f32),
            pltpu.VMEM(block, f32),
            pltpu.VMEM((cells_z, sites * cells_y, cells_x), f32),
            pltpu.VMEM((sites, total_z * SUB, total_y), f32),
            pltpu.VMEM((blocks, SUB, LANES), f32),
            pltpu.VMEM((blocks, up(len(pairs(history))), LANES), f32),
            dma((6,)),
            dma((3 + strips[0],)),
            dma((2,)),
            dma((1,)),
            dma((chunks,)),
            dma((1,)),
            dma((chunks,)),
            dma((1,)),
            dma((cells_z,)),
            dma((4,)),
        ],
        compiler_params=pltpu.CompilerParams(
            collective_id=0, has_side_effects=True, vmem_limit_bytes=39 * 2**20
        ),
        name="iterate",
    )(
        atom_table,
        atom_counts,
        amps,
        widths,
        indirect.reshape(flat),
        indirect.reshape((blocks, cells_z, sites, SUB, cells_x)),
        past_indirect.reshape((history,) + flat),
        past_residual.reshape((history,) + flat),
        jnp.asarray(table_wave),
        jnp.asarray(table_deep),
    )


def blend_kernel(mixing, earlier, residual, now, new_out, residual_out, new, out_sem, copy_sem):
    history = earlier.shape[0]
    strips, cells, _ = residual.shape
    _, blocks, cells_z, sites, _, _ = now.shape
    parts = out_sem.shape[0]
    tall = cells // parts
    inner = [(d, s) for d in range(cells_z) for s in range(sites)]

    def rows(p):
        return slice(p * tall, (p + 1) * tall)

    def strip(n):
        return slice(n * LANES, (n + 1) * LANES)

    copies = [
        pltpu.make_async_copy(residual.at[n], residual_out.at[:, strip(n)], copy_sem.at[n])
        for n in range(strips)
    ]
    for copy in copies:
        copy.start()
    scale = [jnp.broadcast_to(mixing[h : h + 1, :], (SUB, LANES)) for h in range(history + 1)]

    def step(b, carry):
        for t, (d, s) in enumerate(inner):
            place = pl.ds(pl.multiple_of((b * len(inner) + t) * SUB, SUB), SUB)
            for n in range(strips):
                mixed = scale[0] * (now[n, b, d, s] + MIX_STEP * residual[n, place, :])
                for h in range(history):
                    mixed = mixed + scale[h + 1] * earlier[h, n, place, :]
                new[n, place, :] = mixed
        return carry

    stores = []
    for p in range(parts):
        lax.fori_loop(p * blocks // parts, (p + 1) * blocks // parts, step, 0)
        for n in range(strips):
            stores.append(
                pltpu.make_async_copy(
                    new.at[n, rows(p)], new_out.at[rows(p), strip(n)], out_sem.at[p, n]
                )
            )
            stores[-1].start()
    for copy in stores + copies:
        copy.wait()


def blend(mixing, earlier, residual, now):
    strips, cells, _ = residual.shape
    flat = (cells, strips * LANES)
    parts = math.gcd(8, now.shape[1])
    anywhere = pl.BlockSpec(memory_space=pl.ANY)
    vector = pl.BlockSpec(memory_space=pltpu.VMEM)
    dma = pltpu.SemaphoreType.DMA
    held = [
        pltpu.with_memory_space_constraint(value, pltpu.VMEM)
        for value in (mixing, earlier, residual, now)
    ]
    return pl.pallas_call(
        blend_kernel,
        in_specs=[vector] * 4,
        out_specs=[anywhere] * 2,
        out_shape=[jax.ShapeDtypeStruct(flat, jnp.float32)] * 2,
        scratch_shapes=[
            pltpu.VMEM(residual.shape, jnp.float32),
            dma((parts, strips)),
            dma((strips,)),
        ],
        compiler_params=pltpu.CompilerParams(vmem_limit_bytes=12 * 2**20),
        name="blend",
    )(*held)


def body(indirect, past_indirect, past_residual, atom_table, atom_counts, chi_amps, chi_widths):
    cells_y = indirect.shape[1]
    cells_z = indirect.shape[2]
    cells_x = indirect.shape[3]
    parts_y = lax.axis_size("gy")
    parts_z = lax.axis_size("gz")
    total_y = cells_y * parts_y
    total_z = cells_z * parts_z
    row_count = atom_table.shape[3]
    sizes = (
        parts_y, parts_z, indirect.shape[0], cells_y, cells_z, cells_x, past_residual.shape[0]
    )
    if fits(sizes, row_count):
        held = iterate(
            sizes,
            indirect,
            past_indirect,
            past_residual,
            atom_table,
            atom_counts,
            chi_amps,
            chi_widths,
        )
        return tuple(output.reshape(indirect.shape) for output in blend(*held))
    present = (lax.iota(jnp.int32, row_count) < atom_counts[0, 0]).astype(jnp.float32)
    bucket = jnp.concatenate([atom_table[0:3], atom_table[3:5] * present], 0)
    nearby = with_halo(bucket, (("gy", 1), ("gz", 2)), 1)
    nearby = nearby.reshape(5, 9 * row_count)
    potential_field = pencil_field(
        nearby,
        lax.axis_index("gy"),
        lax.axis_index("gz"),
        cells_y,
        cells_z,
        cells_x,
        total_y,
        total_z,
        float(SIGX),
    )
    potential_field = potential_field.reshape(2, cells_y, cells_z, cells_x)
    argument = indirect - potential_field
    closed = jnp.where(argument > 0, argument, jnp.expm1(jnp.minimum(argument, 0.0)))
    direct = closed - indirect
    table_x = hartley(cells_x)
    table_y = hartley(total_y)
    table_z = hartley(total_z)
    blocks = parts_y * parts_z
    width_x = cells_x // blocks
    grid_y = table_y.reshape(parts_y, cells_y, total_y)
    grid_z = table_z.reshape(parts_z, cells_z, total_z)
    outgoing = jnp.einsum(
        "scdx,xqk->qsdkc", direct, table_x.reshape(cells_x, blocks, width_x), precision=PRECISE
    )
    received = lax.all_to_all(outgoing, ("gy", "gz"), split_axis=0, concat_axis=0, tiled=True)
    wave_x = wave_squared(
        lax.axis_index(("gy", "gz")) * width_x + lax.iota(jnp.int32, width_x), cells_x
    )
    wave_square = (
        wave_x[:, None, None]
        + wave_squared(lax.iota(jnp.int32, total_z), total_z)[None, :, None]
        + wave_squared(lax.iota(jnp.int32, total_y), total_y)[None, None, :]
    )
    oxygen, mixed_site, hydrogen = lax.optimization_barrier(
        response(wave_square, chi_amps, chi_widths)
    )
    pieces = received.reshape(parts_y, parts_z, 2, cells_z, width_x, cells_y)
    partial_value = jnp.einsum("absdxc,acy->sbxdy", pieces, grid_y, precision=PRECISE)
    spectrum = jnp.einsum("sbxdy,bdz->sxzy", partial_value, grid_z, precision=PRECISE)
    coupled = jnp.stack(
        [
            oxygen * spectrum[0] + mixed_site * spectrum[1],
            mixed_site * spectrum[0] + hydrogen * spectrum[1],
        ]
    )
    partial_value = jnp.einsum("sxzy,bdz->sxbdy", coupled, grid_z, precision=PRECISE)
    returning = jnp.einsum("sxbdy,acy->absdxc", partial_value, grid_y, precision=PRECISE)
    returning = returning.reshape(blocks, 2, cells_z, width_x, cells_y)
    earlier = past_indirect + MIX_STEP * past_residual
    table_back = table_x.reshape(blocks, width_x, cells_x)
    received = lax.all_to_all(returning, ("gy", "gz"), split_axis=0, concat_axis=0, tiled=True)
    received, earlier = lax.optimization_barrier((received, earlier))
    total = jnp.einsum("qsdxc,qxk->sdck", received, table_back, precision=PRECISE)
    residual, products = finish(total, direct, indirect, past_residual)
    products = everywhere(jnp.sum(products, axis=(1, 2)), ("gy", "gz"))
    count = past_residual.shape[0] + 1
    where = {pair: n for n, pair in enumerate(pairs(count))}
    gram_matrix = jnp.stack(
        [products[where[min(i, j), max(i, j)]] for i in range(count) for j in range(count)]
    ).reshape(count, count)
    factor = jnp.linalg.cholesky(gram_matrix)
    weights = jax.scipy.linalg.cho_solve((factor, True), jnp.ones((count,), jnp.float32))
    mixing = weights / jnp.sum(weights)
    new_indirect = mix(mixing, indirect, residual, earlier)
    return (new_indirect, residual)


def solution(mesh):
    return jax.shard_map(
        body,
        mesh=mesh,
        in_specs=(
            P("groups", "gy", "gz", None),
            P("groups", None, "gy", "gz", None),
            P("groups", None, "gy", "gz", None),
            P("groups", "gy", "gz", None),
            P(("groups", "gy"), "gz"),
            P(),
            P(),
        ),
        out_specs=(P("groups", "gy", "gz", None), P("groups", "gy", "gz", None)),
        check_vma=False,
    )
```

```python
import functools
import math

import jax
import jax.numpy as jnp
import ml_dtypes
import numpy as np
from jax import lax
from jax.experimental import pallas as pl
from jax.experimental.pallas import tpu as pltpu
from jax.sharding import PartitionSpec as P

SIGX = 8


PRECISE = lax.Precision.HIGH
MIX_STEP = 0.3
BOND_OH = 1.9
BOND_HH = 3.1


def with_halo(cells, sides, width):
    for axis, dim in sides:
        count = lax.axis_size(axis)
        head = lax.slice_in_dim(cells, 0, width, axis=dim)
        tail = lax.slice_in_dim(cells, cells.shape[dim] - width, cells.shape[dim], axis=dim)
        cells = jnp.concatenate(
            [
                lax.ppermute(tail, axis, [(i, (i + 1) % count) for i in range(count)]),
                cells,
                lax.ppermute(head, axis, [((i + 1) % count, i) for i in range(count)]),
            ],
            axis=dim,
        )
    return cells


def hartley(length):
    position = lax.iota(jnp.int32, length)
    product = position[:, None] * position[None, :] % length
    angle = product.astype(jnp.float32) * (2.0 * math.pi / length)
    return (jnp.cos(angle) + jnp.sin(angle)) / math.sqrt(length)


def wave_squared(position, length):
    folded = jnp.where(2 * position > length, position - length, position)
    scaled = folded.astype(jnp.float32) * (2.0 * math.pi / length)
    return scaled * scaled


def response(wave_square, chi_amps, chi_widths):
    wavenumber = jnp.sqrt(wave_square)
    summed = [jnp.zeros_like(wave_square) for channel in range(3)]
    for which_term in range(chi_widths.shape[0]):
        gaussian_term = jnp.exp(-wave_square * (chi_widths[which_term] * chi_widths[which_term]))
        summed = [
            summed[channel] + chi_amps[channel, which_term] * gaussian_term for channel in range(3)
        ]
    oxygen = 1.0 + summed[0]
    mixed_site = 2.0 * jnp.sinc(wavenumber * (BOND_OH / math.pi)) + summed[1]
    hydrogen = 2.0 + 2.0 * jnp.sinc(wavenumber * (BOND_HH / math.pi)) + summed[2]
    return (oxygen, mixed_site, hydrogen)


def gaussian(offset, length, spread):
    offset = offset - length * jnp.floor(offset / length + 0.5)
    return jnp.exp(-0.5 * offset * offset / (spread * spread))


def pencil_field(
    atom_rows, pencil_y, pencil_z, cells_y, cells_z, total_x, total_y, total_z, spread_x
):
    cell_y = (pencil_y * cells_y + lax.iota(jnp.int32, cells_y)).astype(jnp.float32)
    cell_z = (pencil_z * cells_z + lax.iota(jnp.int32, cells_z)).astype(jnp.float32)
    cell_x = lax.iota(jnp.int32, total_x).astype(jnp.float32)
    along_y = gaussian(cell_y[:, None] - atom_rows[1][None, :], total_y, 0.5 * cells_y)
    along_z = gaussian(cell_z[:, None] - atom_rows[2][None, :], total_z, 0.5 * cells_z)
    along_x = gaussian(cell_x[:, None] - atom_rows[0][None, :], total_x, spread_x)
    left = atom_rows[3:5][:, None, None, :] * along_y[None, :, None, :] * along_z[None, None, :, :]
    left = left.reshape(2, cells_y * cells_z, atom_rows.shape[1])
    return jnp.einsum("sra,xa->srx", left, along_x, precision=PRECISE)


def pairs(count):
    return [(i, j) for i in range(count) for j in range(i, count)]


def everywhere(value, axes):
    for axis in axes:
        size = lax.axis_size(axis)
        if size & (size - 1):
            value = lax.psum(value, axis)
            continue
        step = 1
        while step < size:
            value = value + lax.ppermute(value, axis, [(i, i ^ step) for i in range(size)])
            step *= 2
    return value


def finish_kernel(total, direct, indirect, past, residual, products):
    history, _, rows, _, cells_x = past.shape
    couples = pairs(history + 1)

    @pl.when((pl.program_id(0) == 0) & (pl.program_id(1) == 0))
    def _():
        products[...] = jnp.zeros_like(products)

    lanes = products.shape[2]
    sums = tuple(products[n] for n in range(len(couples)))
    for lane in range(0, cells_x, lanes):
        columns = pl.ds(lane, lanes)

        def step(group, sums):
            first = pl.multiple_of(group * 8, 8)
            turned = jnp.swapaxes(total[0, :, pl.ds(first, 8), columns], 0, 1)
            for offset in range(8):
                row = first + offset
                now = turned[offset] - direct[0, row, :, columns] - indirect[0, row, :, columns]
                residual[0, row, :, columns] = now
                values = [now] + [past[h, 0, row, :, columns] for h in range(history)]
                sums = tuple(
                    sums[n] + values[i] * values[j] for n, (i, j) in enumerate(couples)
                )
            return sums

        sums = lax.fori_loop(0, rows // 8, step, sums)
    for n in range(len(couples)):
        products[n] = sums[n]


def block_rows(cells_y):
    return math.gcd(cells_y, 32)


def finish(total, direct, indirect, past_residual):
    history, sites, cells_y, cells_z, cells_x = past_residual.shape
    rows = block_rows(cells_y)
    field = pl.BlockSpec((1, rows, cells_z, cells_x), lambda s, c: (s, c, 0, 0))
    earlier = pl.BlockSpec((history, 1, rows, cells_z, cells_x), lambda s, c: (0, s, c, 0, 0))
    count = len(pairs(history + 1))
    lanes = min(cells_x, 128)
    return pl.pallas_call(
        finish_kernel,
        grid=(sites, cells_y // rows),
        in_specs=[
            pl.BlockSpec((1, cells_z, rows, cells_x), lambda s, c: (s, 0, c, 0)),
            field,
            field,
            earlier,
        ],
        out_specs=[field, pl.BlockSpec((count, cells_z, lanes), lambda s, c: (0, 0, 0))],
        out_shape=[
            jax.ShapeDtypeStruct(indirect.shape, jnp.float32),
            jax.ShapeDtypeStruct((count, cells_z, lanes), jnp.float32),
        ],
        name="finish",
    )(total, direct, indirect, past_residual)


def mix_kernel(mixing, indirect, residual, earlier, out):
    history = earlier.shape[0]
    rows = indirect.shape[1]
    scale = [mixing[h] for h in range(history + 1)]

    def step(row, carry):
        mixed = scale[0] * (indirect[0, row] + MIX_STEP * residual[0, row])
        for h in range(history):
            mixed = mixed + scale[h + 1] * earlier[h, 0, row]
        out[0, row] = mixed
        return carry

    lax.fori_loop(0, rows, step, 0, unroll=2)


def mix(mixing, indirect, residual, earlier):
    history, sites, cells_y, cells_z, cells_x = earlier.shape
    rows = block_rows(cells_y)
    field = pl.BlockSpec((1, rows, cells_z, cells_x), lambda s, c: (s, c, 0, 0))
    stack = pl.BlockSpec((history, 1, rows, cells_z, cells_x), lambda s, c: (0, s, c, 0, 0))
    return pl.pallas_call(
        mix_kernel,
        grid=(sites, cells_y // rows),
        in_specs=[pl.BlockSpec(memory_space=pltpu.SMEM), field, field, stack],
        out_specs=field,
        out_shape=jax.ShapeDtypeStruct(indirect.shape, jnp.float32),
        name="mix",
    )(mixing, indirect, residual, earlier)


def folded_angle(position, length):
    folded = jnp.where(2 * position > length, position - length, position)
    return folded.astype(jnp.float32) * (2.0 * math.pi / length)


def halves(value):
    high = value.astype(jnp.bfloat16)
    return high, (value - high.astype(jnp.float32)).astype(jnp.bfloat16)


def table_halves(table):
    high = table.astype(ml_dtypes.bfloat16)
    return high, (table - high.astype(np.float32)).astype(ml_dtypes.bfloat16)


def product(left, right, dims=(1, 0)):
    numbers = (((dims[0],), (dims[1],)), ((), ()))

    def dot(a, b):
        return lax.dot_general(a, b, numbers, preferred_element_type=jnp.float32)

    return dot(left[0], right[0]) + (dot(left[0], right[1]) + dot(left[1], right[0]))


def host_hartley(length):
    position = np.arange(length)
    angle = (position[:, None] * position[None, :] % length) * (2.0 * math.pi / length)
    return ((np.cos(angle) + np.sin(angle)) / math.sqrt(length)).astype(np.float32)


def sine_over(v):
    turns = jnp.floor(v * (1.0 / math.pi) + 0.5)
    r = (v - turns * 3.140625) - turns * (math.pi - 3.140625)
    odd = turns - 2.0 * jnp.floor(0.5 * turns)
    r2 = r * r
    series = -2.5052108e-08
    for term in (2.7557319e-06, -1.9841270e-04, 8.3333333e-03, -1.6666667e-01):
        series = series * r2 + term
    sine = (r + r * r2 * series) * (1.0 - 2.0 * odd)
    return jnp.where(v == 0.0, 1.0, sine / jnp.where(v == 0.0, 1.0, v))


def solve_ones(gram, count):
    rows = [[gram[min(i, j), max(i, j)] for j in range(count)] for i in range(count)]
    right = [jnp.ones_like(rows[0][0]) for i in range(count)]
    for k in range(count):
        inverse = 1.0 / rows[k][k]
        for i in range(k + 1, count):
            factor = rows[k][i] * inverse
            for j in range(i, count):
                rows[i][j] = rows[i][j] - factor * rows[k][j]
            right[i] = right[i] - factor * right[k]
    weights = [None] * count
    for k in reversed(range(count)):
        value = right[k]
        for j in range(k + 1, count):
            value = value - rows[k][j] * weights[j]
        weights[k] = value / rows[k][k]
    total = weights[0]
    for k in range(1, count):
        total = total + weights[k]
    return [weight / total for weight in weights]


SUB = 8
LANES = 128


def bell(offset, length, spread):
    offset = offset - length * jnp.floor(offset * (1.0 / length) + 0.5)
    return jnp.exp(offset * offset * (-0.5 / (spread * spread)))


def iterate_kernel(
    sizes,
    atoms_in,
    live_in,
    amps_in,
    widths_in,
    indirect,
    indirect_tiles,
    past_indirect,
    past_residual,
    table_wave,
    table_deep,
    mixing_out,
    earlier,
    field,
    outgoing,
    atoms,
    live,
    amps,
    widths,
    near,
    wave,
    deep_wave,
    grid_x,
    grid_y,
    old,
    planes,
    returned,
    total,
    spectrum,
    sums,
    sums_past,
    small_sem,
    load_sem,
    near_sem,
    go_send,
    go_recv,
    back_send,
    back_recv,
    last_send,
    last_recv,
    sum_sem,
):
    parts_y, parts_z, sites, cells_y, cells_z, cells_x, history = sizes
    total_y, total_z = parts_y * cells_y, parts_z * cells_z
    blocks = parts_y * parts_z
    chunks = cells_x // blocks // SUB
    lines = sites * cells_y
    strips = cells_x // LANES
    cells = lines * cells_z
    group = lax.axis_index("groups")
    my_y = lax.axis_index("gy")
    my_z = lax.axis_index("gz")
    me = my_y * parts_z + my_z

    def device(q):
        return (group, q // parts_z, q % parts_z)

    def remote(source, target, send, receive, q):
        return pltpu.make_async_remote_copy(
            src_ref=source,
            dst_ref=target,
            send_sem=send,
            recv_sem=receive,
            device_id=device(q),
            device_id_type=pl.DeviceIdType.MESH,
        )

    def each_partner(do):
        def step(i, carry):
            do((me + i) % blocks)
            return carry

        lax.fori_loop(1, blocks, step, 0)

    def strip(n):
        return slice(n * LANES, (n + 1) * LANES)

    def taken(ref, sem):
        pltpu.make_async_copy(ref, ref, sem).wait()

    first = [
        pltpu.make_async_copy(atoms_in, atoms, small_sem.at[0]),
        pltpu.make_async_copy(live_in, live, small_sem.at[1]),
        pltpu.make_async_copy(amps_in, amps, small_sem.at[2]),
        pltpu.make_async_copy(widths_in, widths, small_sem.at[3]),
        pltpu.make_async_copy(table_wave, wave, small_sem.at[4]),
        pltpu.make_async_copy(table_deep, deep_wave, small_sem.at[5]),
    ]
    for copy in first:
        copy.start()
    for n in range(strips):
        pltpu.make_async_copy(indirect.at[:, strip(n)], field.at[n], load_sem.at[0]).start()

    barrier = pltpu.get_barrier_semaphore()
    each_partner(
        lambda q: pl.semaphore_signal(
            barrier, inc=1, device_id=device(q), device_id_type=pl.DeviceIdType.MESH
        )
    )

    rows = atoms.shape[3]
    for copy in first[:2]:
        copy.wait()
    present = jnp.where(lax.broadcasted_iota(jnp.int32, (1, rows), 1) < live[0, 0], 1.0, 0.0)
    near[4] = jnp.zeros((SUB, rows), jnp.float32)
    for n in range(5):
        row = atoms[n, 0]
        near[4, n : n + 1, :] = row * present if n >= 3 else row
    pl.semaphore_wait(barrier, blocks - 1)

    shifts = [(a, b) for a in (-1, 0, 1) for b in (-1, 0, 1)]
    for n, (a, b) in enumerate(shifts):
        if (a, b) != (0, 0):
            q = ((my_y + a + parts_y) % parts_y) * parts_z + (my_z + b + parts_z) % parts_z
            slot = len(shifts) - 1 - n
            remote(near.at[4], near.at[slot], near_sem.at[0], near_sem.at[1], q).start()

    cell_x = lax.broadcasted_iota(jnp.int32, (cells_x, rows), 0).astype(jnp.float32)
    cell_y = (
        my_y * cells_y + lax.broadcasted_iota(jnp.int32, (cells_y, rows), 0)
    ).astype(jnp.float32)

    def spread_atoms(n):
        columns = slice(n * rows, (n + 1) * rows)
        along_x = bell(cell_x - near[n, 0:1, :], cells_x, float(SIGX))
        high, low = halves(along_x)
        grid_x[0, :, columns] = high
        grid_x[1, :, columns] = low
        grid_y[:, columns] = bell(cell_y - near[n, 1:2, :], total_y, 0.5 * cells_y)

    spread_atoms(4)
    taken(near.at[0 : len(shifts) - 1], near_sem.at[1])
    for n in range(len(shifts)):
        if n != 4:
            spread_atoms(n)
    first[4].wait()
    taken(field, load_sem.at[0])
    place_z = jnp.concatenate([near[n, 2:3, :] for n in range(len(shifts))], 1)
    strength = [
        jnp.concatenate([near[n, 3 + s : 4 + s, :] for n in range(len(shifts))], 1)
        for s in range(sites)
    ]

    def go(j, q):
        return remote(
            outgoing.at[j, q], planes.at[j, me], go_send.at[0], go_recv.at[j], q
        )

    def go_first(d, q):
        return remote(
            outgoing.at[0, q, d], planes.at[0, me, d], go_send.at[0], go_recv.at[0], q
        )

    def own(j):
        return pltpu.make_async_copy(outgoing.at[j, me], planes.at[j, me], go_recv.at[j])

    def slab(d, carry):
        here_z = (my_z * cells_z + d).astype(jnp.float32)
        along_z = bell(here_z - place_z, total_z, 0.5 * cells_z)
        left = jnp.concatenate([grid_y[...] * (strength[s] * along_z) for s in range(sites)], 0)
        potential = product(halves(left), (grid_x[0], grid_x[1]), (1, 1))
        now = jnp.concatenate(
            [field[n, pl.ds(d, lines, stride=cells_z), :] for n in range(strips)], 1
        )
        argument = now - potential
        closed = jnp.where(argument > 0, argument, jnp.exp(jnp.minimum(argument, 0.0)) - 1.0)
        total[d] = -closed
        waves = product((wave[0], wave[1]), halves(closed - now), (1, 1))
        for s in range(sites):
            part = waves[:, s * cells_y : (s + 1) * cells_y]
            outgoing[:, :, d, s] = part.reshape(chunks, blocks, SUB, cells_y)
        each_partner(lambda q: go_first(d, q).start())
        return carry

    lax.fori_loop(0, cells_z, slab, 0)
    for n in (2, 3, 5):
        first[n].wait()
    for h in range(history):
        for n in range(strips):
            pltpu.make_async_copy(
                past_residual.at[h, :, strip(n)], old.at[h, n], load_sem.at[1]
            ).start()
            pltpu.make_async_copy(
                past_indirect.at[h, :, strip(n)], earlier.at[h, n], load_sem.at[2]
            ).start()
    own(0).start()

    def issue(j, carry):
        own(j).start()
        each_partner(lambda q: go(j, q).start())
        return carry

    lax.fori_loop(1, chunks, issue, 0)

    taken(old, load_sem.at[1])
    taken(earlier, load_sem.at[2])
    couples = pairs(history)

    def stripe(t, acc):
        place = pl.ds(pl.multiple_of(t * SUB, SUB), SUB)
        acc = list(acc)
        for n in range(strips):
            values = [old[h, n, place, :] for h in range(history)]
            for h in range(history):
                earlier[h, n, place, :] = earlier[h, n, place, :] + MIX_STEP * values[h]
            for c, (i, j) in enumerate(couples):
                acc[c] = acc[c] + values[i] * values[j]
        return tuple(acc)

    zero = jnp.zeros((SUB, LANES), jnp.float32)
    acc = lax.fori_loop(0, cells // SUB, stripe, tuple(zero for _ in couples))

    def put(target, values):
        target[me] = jnp.zeros(target.shape[1:], jnp.float32)
        for n, value in enumerate(values):
            target[me, n : n + 1, :] = jnp.sum(value, 0, keepdims=True)

    def share(tiles, which):
        each_partner(
            lambda q: remote(
                tiles.at[me], tiles.at[me], sum_sem.at[2 * which], sum_sem.at[2 * which + 1], q
            ).start()
        )

    def all_sums(tiles, which):
        taken(tiles.at[0 : blocks - 1], sum_sem.at[2 * which + 1])
        whole = jnp.sum(jnp.sum(tiles[...], 0), 1, keepdims=True)
        return jnp.broadcast_to(whole, tiles.shape[1:])

    put(sums_past, acc)
    share(sums_past, 0)

    def couple_step(t, j):
        tall_z = 4 * SUB
        first = pl.multiple_of(t * tall_z, tall_z)
        row = lax.broadcasted_iota(jnp.int32, (tall_z, total_y), 0)
        angle_z = folded_angle((first + row) // SUB, total_z)
        angle_x = folded_angle((j * blocks + me) * SUB + row % SUB, cells_x)
        angle_y = folded_angle(lax.broadcasted_iota(jnp.int32, (tall_z, total_y), 1), total_y)
        square = angle_x * angle_x + angle_z * angle_z + angle_y * angle_y
        number = jnp.sqrt(square)
        oxygen = jnp.ones_like(square)
        mixed = 2.0 * sine_over(number * BOND_OH)
        hydrogen = 2.0 + 2.0 * sine_over(number * BOND_HH)
        for term in range(widths.shape[0]):
            decay = jnp.exp(-square * (widths[term] * widths[term]))
            oxygen = oxygen + amps[0, term] * decay
            mixed = mixed + amps[1, term] * decay
            hydrogen = hydrogen + amps[2, term] * decay
        at = pl.ds(first, tall_z)
        first_site, second_site = spectrum[0, at, :], spectrum[1, at, :]
        spectrum[0, at, :] = oxygen * first_site + mixed * second_site
        spectrum[1, at, :] = mixed * first_site + hydrogen * second_site
        return j

    deep = total_z * SUB

    def middle(j):
        along_y = (wave[0], wave[1])
        along_z = (deep_wave[0], deep_wave[1])
        for s in range(sites):
            plane = jnp.concatenate(
                [
                    planes[j, a * parts_z : (a + 1) * parts_z, :, s].reshape(deep, cells_y)
                    for a in range(parts_y)
                ],
                1,
            )
            plane = product(halves(plane), along_y)
            spectrum[s] = product(along_z, halves(plane))
        lax.fori_loop(0, deep // (4 * SUB), couple_step, j)
        for s in range(sites):
            plane = product(along_z, halves(spectrum[s]))
            plane = product(halves(plane), along_y)
            for a in range(parts_y):
                part = plane[:, a * cells_y : (a + 1) * cells_y]
                planes[j, a * parts_z : (a + 1) * parts_z, :, s] = part.reshape(
                    parts_z, cells_z, SUB, cells_y
                )

    last = chunks - 1

    def back(j, q):
        return remote(
            planes.at[j, q], returned.at[j, me], back_send.at[0], back_recv.at[j], q
        )

    def back_self(j):
        return pltpu.make_async_copy(planes.at[j, me], returned.at[j, me], back_recv.at[j])

    def back_last(d, q):
        return remote(
            planes.at[last, q, d],
            returned.at[last, me, d],
            last_send.at[0],
            last_recv.at[d],
            q,
        )

    def last_self(d):
        return pltpu.make_async_copy(
            planes.at[last, me, d], returned.at[last, me, d], last_recv.at[d]
        )

    def middle_step(j, carry):
        taken(planes.at[j], go_recv.at[j])
        middle(j)

        @pl.when(j < last)
        def _():
            back_self(j).start()
            each_partner(lambda q: back(j, q).start())

        return carry

    lax.fori_loop(0, chunks, middle_step, 0)

    def send_last(d, carry):
        last_self(d).start()
        each_partner(lambda q: back_last(d, q).start())
        return carry

    lax.fori_loop(0, cells_z, send_last, 0)

    def lines_of(j, d):
        waves = jnp.concatenate(
            [returned[j, :, d, s].reshape(blocks * SUB, cells_y) for s in range(sites)], 1
        )
        here = pl.ds(pl.multiple_of(j * blocks * SUB, blocks * SUB), blocks * SUB)
        return product(halves(waves.T), (wave[0, here, :], wave[1, here, :]))

    def home(j, carry):
        taken(returned.at[j], back_recv.at[j])

        def slab_back(d, carry):
            total[d] = total[d] + lines_of(j, d)
            return carry

        return lax.fori_loop(0, cells_z, slab_back, carry)

    lax.fori_loop(0, last, home, 0)

    known = all_sums(sums_past, 0)
    taken(near.at[0 : len(shifts) - 1], near_sem.at[0])
    taken(sums_past.at[0 : blocks - 1], sum_sem.at[0])
    taken(outgoing.at[:, 0 : blocks - 1], go_send.at[0])
    taken(planes.at[0:last, 0 : blocks - 1], back_send.at[0])
    again = [
        pltpu.make_async_copy(
            indirect_tiles.at[:, :, :, :, strip(n)], outgoing.at[n], load_sem.at[3 + n]
        )
        for n in range(strips)
    ]
    for copy in again:
        copy.start()

    def slab_last(d, acc):
        taken(returned.at[last, :, d], last_recv.at[d])
        new = total[d] + lines_of(last, d)
        acc = list(acc)
        for n in range(strips):
            place = pl.ds(d, lines, stride=cells_z)
            now = new[:, strip(n)]
            field[n, place, :] = now
            for h in range(history + 1):
                both = now * (now if h == 0 else old[h - 1, n, place, :])
                acc[h] = acc[h] + jnp.sum(both.reshape(lines // SUB, SUB, LANES), 0)
        return tuple(acc)

    acc = lax.fori_loop(0, cells_z, slab_last, tuple(zero for _ in range(history + 1)))
    put(sums, acc)
    share(sums, 1)
    taken(planes.at[last, 0 : blocks - 1], last_send.at[0])
    fresh = all_sums(sums, 1)
    gram = {(0, i): fresh[i : i + 1, :] for i in range(history + 1)}
    for n, (i, j) in enumerate(couples):
        gram[i + 1, j + 1] = known[n : n + 1, :]
    for n, value in enumerate(solve_ones(gram, history + 1)):
        mixing_out[n : n + 1, :] = value
    mixing_out[history + 1 :, :] = jnp.zeros(
        (mixing_out.shape[0] - history - 1, LANES), jnp.float32
    )
    taken(sums.at[0 : blocks - 1], sum_sem.at[2])
    for copy in again:
        copy.wait()


def fits(sizes, rows):
    parts_y, parts_z, sites, cells_y, cells_z, cells_x, history = sizes
    blocks = parts_y * parts_z
    return (
        min(parts_y, parts_z) >= 3
        and sites == 2
        and cells_y == LANES
        and cells_z % SUB == 0
        and cells_x == parts_y * cells_y
        and cells_x % LANES == 0
        and blocks * SUB == LANES
        and rows % LANES == 0
        and history + 1 <= SUB
        and history * sites * cells_y * cells_z * cells_x * 4 <= 16 * 2**20
    )


def up(count):
    return -(-count // SUB) * SUB


def iterate(sizes, indirect, past_indirect, past_residual, atom_table, atom_counts, amps, widths):
    parts_y, parts_z, sites, cells_y, cells_z, cells_x, history = sizes
    total_y, total_z = parts_y * cells_y, parts_z * cells_z
    blocks = parts_y * parts_z
    chunks = cells_x // blocks // SUB
    rows = atom_table.shape[3]
    table_wave = np.stack(table_halves(host_hartley(cells_x)))
    table_deep = np.stack(
        table_halves(np.kron(host_hartley(total_z), np.eye(SUB, dtype=np.float32)))
    )
    flat = (sites * cells_y * cells_z, cells_x)
    strips = (cells_x // LANES, flat[0], LANES)
    block = (chunks, blocks, cells_z, sites, SUB, cells_y)
    anywhere = pl.BlockSpec(memory_space=pl.ANY)
    vector = pl.BlockSpec(memory_space=pltpu.VMEM)
    dma = pltpu.SemaphoreType.DMA
    f32 = jnp.float32
    b16 = jnp.bfloat16
    return pl.pallas_call(
        functools.partial(iterate_kernel, sizes),
        in_specs=[anywhere] * 10,
        out_specs=[vector] * 4,
        out_shape=[
            pltpu.VMEM((SUB, LANES), f32),
            pltpu.VMEM((history,) + strips, f32),
            pltpu.VMEM(strips, f32),
            pltpu.VMEM(block, f32),
        ],
        scratch_shapes=[
            pltpu.VMEM(atom_table.shape, f32),
            pltpu.SMEM(atom_counts.shape, jnp.int32),
            pltpu.SMEM(amps.shape, f32),
            pltpu.SMEM(widths.shape, f32),
            pltpu.VMEM((9, SUB, rows), f32),
            pltpu.VMEM(table_wave.shape, b16),
            pltpu.VMEM(table_deep.shape, b16),
            pltpu.VMEM((2, cells_x, 9 * rows), b16),
            pltpu.VMEM((cells_y, 9 * rows), f32),
            pltpu.VMEM((history,) + strips, f32),
            pltpu.VMEM(block, f32),
            pltpu.VMEM(block, f32),
            pltpu.VMEM((cells_z, sites * cells_y, cells_x), f32),
            pltpu.VMEM((sites, total_z * SUB, total_y), f32),
            pltpu.VMEM((blocks, SUB, LANES), f32),
            pltpu.VMEM((blocks, up(len(pairs(history))), LANES), f32),
            dma((6,)),
            dma((3 + strips[0],)),
            dma((2,)),
            dma((1,)),
            dma((chunks,)),
            dma((1,)),
            dma((chunks,)),
            dma((1,)),
            dma((cells_z,)),
            dma((4,)),
        ],
        compiler_params=pltpu.CompilerParams(
            collective_id=0, has_side_effects=True, vmem_limit_bytes=39 * 2**20
        ),
        name="iterate",
    )(
        atom_table,
        atom_counts,
        amps,
        widths,
        indirect.reshape(flat),
        indirect.reshape((blocks, cells_z, sites, SUB, cells_x)),
        past_indirect.reshape((history,) + flat),
        past_residual.reshape((history,) + flat),
        jnp.asarray(table_wave),
        jnp.asarray(table_deep),
    )


def blend_kernel(mixing, earlier, residual, now, new_out, residual_out, new, out_sem, copy_sem):
    history = earlier.shape[0]
    strips, cells, _ = residual.shape
    _, blocks, cells_z, sites, _, _ = now.shape
    parts = out_sem.shape[0]
    tall = cells // parts
    inner = [(d, s) for d in range(cells_z) for s in range(sites)]

    def rows(p):
        return slice(p * tall, (p + 1) * tall)

    def strip(n):
        return slice(n * LANES, (n + 1) * LANES)

    copies = [
        pltpu.make_async_copy(residual.at[n], residual_out.at[:, strip(n)], copy_sem.at[n])
        for n in range(strips)
    ]
    for copy in copies:
        copy.start()
    scale = [jnp.broadcast_to(mixing[h : h + 1, :], (SUB, LANES)) for h in range(history + 1)]

    def step(b, carry):
        for t, (d, s) in enumerate(inner):
            place = pl.ds(pl.multiple_of((b * len(inner) + t) * SUB, SUB), SUB)
            for n in range(strips):
                mixed = scale[0] * (now[n, b, d, s] + MIX_STEP * residual[n, place, :])
                for h in range(history):
                    mixed = mixed + scale[h + 1] * earlier[h, n, place, :]
                new[n, place, :] = mixed
        return carry

    stores = []
    for p in range(parts):
        lax.fori_loop(p * blocks // parts, (p + 1) * blocks // parts, step, 0)
        for n in range(strips):
            stores.append(
                pltpu.make_async_copy(
                    new.at[n, rows(p)], new_out.at[rows(p), strip(n)], out_sem.at[p, n]
                )
            )
            stores[-1].start()
    for copy in stores + copies:
        copy.wait()


def blend(mixing, earlier, residual, now):
    strips, cells, _ = residual.shape
    flat = (cells, strips * LANES)
    parts = math.gcd(4, now.shape[1])
    anywhere = pl.BlockSpec(memory_space=pl.ANY)
    vector = pl.BlockSpec(memory_space=pltpu.VMEM)
    dma = pltpu.SemaphoreType.DMA
    held = [
        pltpu.with_memory_space_constraint(value, pltpu.VMEM)
        for value in (mixing, earlier, residual, now)
    ]
    return pl.pallas_call(
        blend_kernel,
        in_specs=[vector] * 4,
        out_specs=[anywhere] * 2,
        out_shape=[jax.ShapeDtypeStruct(flat, jnp.float32)] * 2,
        scratch_shapes=[
            pltpu.VMEM(residual.shape, jnp.float32),
            dma((parts, strips)),
            dma((strips,)),
        ],
        compiler_params=pltpu.CompilerParams(vmem_limit_bytes=12 * 2**20),
        name="blend",
    )(*held)


def body(indirect, past_indirect, past_residual, atom_table, atom_counts, chi_amps, chi_widths):
    cells_y = indirect.shape[1]
    cells_z = indirect.shape[2]
    cells_x = indirect.shape[3]
    parts_y = lax.axis_size("gy")
    parts_z = lax.axis_size("gz")
    total_y = cells_y * parts_y
    total_z = cells_z * parts_z
    row_count = atom_table.shape[3]
    sizes = (
        parts_y, parts_z, indirect.shape[0], cells_y, cells_z, cells_x, past_residual.shape[0]
    )
    if fits(sizes, row_count):
        held = iterate(
            sizes,
            indirect,
            past_indirect,
            past_residual,
            atom_table,
            atom_counts,
            chi_amps,
            chi_widths,
        )
        return tuple(output.reshape(indirect.shape) for output in blend(*held))
    present = (lax.iota(jnp.int32, row_count) < atom_counts[0, 0]).astype(jnp.float32)
    bucket = jnp.concatenate([atom_table[0:3], atom_table[3:5] * present], 0)
    nearby = with_halo(bucket, (("gy", 1), ("gz", 2)), 1)
    nearby = nearby.reshape(5, 9 * row_count)
    potential_field = pencil_field(
        nearby,
        lax.axis_index("gy"),
        lax.axis_index("gz"),
        cells_y,
        cells_z,
        cells_x,
        total_y,
        total_z,
        float(SIGX),
    )
    potential_field = potential_field.reshape(2, cells_y, cells_z, cells_x)
    argument = indirect - potential_field
    closed = jnp.where(argument > 0, argument, jnp.expm1(jnp.minimum(argument, 0.0)))
    direct = closed - indirect
    table_x = hartley(cells_x)
    table_y = hartley(total_y)
    table_z = hartley(total_z)
    blocks = parts_y * parts_z
    width_x = cells_x // blocks
    grid_y = table_y.reshape(parts_y, cells_y, total_y)
    grid_z = table_z.reshape(parts_z, cells_z, total_z)
    outgoing = jnp.einsum(
        "scdx,xqk->qsdkc", direct, table_x.reshape(cells_x, blocks, width_x), precision=PRECISE
    )
    received = lax.all_to_all(outgoing, ("gy", "gz"), split_axis=0, concat_axis=0, tiled=True)
    wave_x = wave_squared(
        lax.axis_index(("gy", "gz")) * width_x + lax.iota(jnp.int32, width_x), cells_x
    )
    wave_square = (
        wave_x[:, None, None]
        + wave_squared(lax.iota(jnp.int32, total_z), total_z)[None, :, None]
        + wave_squared(lax.iota(jnp.int32, total_y), total_y)[None, None, :]
    )
    oxygen, mixed_site, hydrogen = lax.optimization_barrier(
        response(wave_square, chi_amps, chi_widths)
    )
    pieces = received.reshape(parts_y, parts_z, 2, cells_z, width_x, cells_y)
    partial_value = jnp.einsum("absdxc,acy->sbxdy", pieces, grid_y, precision=PRECISE)
    spectrum = jnp.einsum("sbxdy,bdz->sxzy", partial_value, grid_z, precision=PRECISE)
    coupled = jnp.stack(
        [
            oxygen * spectrum[0] + mixed_site * spectrum[1],
            mixed_site * spectrum[0] + hydrogen * spectrum[1],
        ]
    )
    partial_value = jnp.einsum("sxzy,bdz->sxbdy", coupled, grid_z, precision=PRECISE)
    returning = jnp.einsum("sxbdy,acy->absdxc", partial_value, grid_y, precision=PRECISE)
    returning = returning.reshape(blocks, 2, cells_z, width_x, cells_y)
    earlier = past_indirect + MIX_STEP * past_residual
    table_back = table_x.reshape(blocks, width_x, cells_x)
    received = lax.all_to_all(returning, ("gy", "gz"), split_axis=0, concat_axis=0, tiled=True)
    received, earlier = lax.optimization_barrier((received, earlier))
    total = jnp.einsum("qsdxc,qxk->sdck", received, table_back, precision=PRECISE)
    residual, products = finish(total, direct, indirect, past_residual)
    products = everywhere(jnp.sum(products, axis=(1, 2)), ("gy", "gz"))
    count = past_residual.shape[0] + 1
    where = {pair: n for n, pair in enumerate(pairs(count))}
    gram_matrix = jnp.stack(
        [products[where[min(i, j), max(i, j)]] for i in range(count) for j in range(count)]
    ).reshape(count, count)
    factor = jnp.linalg.cholesky(gram_matrix)
    weights = jax.scipy.linalg.cho_solve((factor, True), jnp.ones((count,), jnp.float32))
    mixing = weights / jnp.sum(weights)
    new_indirect = mix(mixing, indirect, residual, earlier)
    return (new_indirect, residual)


def solution(mesh):
    return jax.shard_map(
        body,
        mesh=mesh,
        in_specs=(
            P("groups", "gy", "gz", None),
            P("groups", None, "gy", "gz", None),
            P("groups", None, "gy", "gz", None),
            P("groups", "gy", "gz", None),
            P(("groups", "gy"), "gz"),
            P(),
            P(),
        ),
        out_specs=(P("groups", "gy", "gz", None), P("groups", "gy", "gz", None)),
        check_vma=False,
    )
```
